128 devices in a mesh: seq: 16 (over x_lo, y, core), tp: 8 (over z, x_hi).
Axes of the slice: x: 4 (x_hi: 2, x_lo: 2; x = x_hi * 2 + x_lo), y: 4, z: 4, core: 2. Of those that a mesh axis runs over, the one named last changes fastest.
Arguments:
- selected_hidden: bfloat16 [32, 104, 2048], P('seq', None, 'tp'), may hold values from -6 to 6
- cached_keys: bfloat16 [32, 1024, 1024], P('seq', None, 'tp'), may hold values from -48 to 48
- cached_values: bfloat16 [32, 1024, 1024], P('seq', None, 'tp'), may hold values from -6 to 6
- slot_spans: int32 [32], replicated, may hold values from 0 to 31, each once
- span_order: int32 [4, 8], replicated, may hold values from 0 to 7, each once within a row
- cache_start: int32 [4, 8], replicated, may hold values from 0 to 16383
- selected_index: int32 [32, 104], replicated, may hold values from 0 to 1023, as said below
- input_gain: bfloat16 [2048], replicated, may hold values from 0.5 to 2
- query_weight: bfloat16 [2048, 2048], P(None, 'tp'), may hold values from -0.125 to 0.125
- key_weight: bfloat16 [2048, 1024], P(None, 'tp'), may hold values from -0.125 to 0.125
- value_weight: bfloat16 [2048, 1024], P(None, 'tp'), may hold values from -0.125 to 0.125
- query_gain: bfloat16 [128], replicated, may hold values from 1 to 2
- key_gain: bfloat16 [128], replicated, may hold values from 1 to 2
- output_weight: bfloat16 [2048, 2048], P('tp'), may hold values from -0.125 to 0.125
- post_gain: bfloat16 [2048], replicated, may hold values from 0.5 to 2
- gate_weight: bfloat16 [2048, 6144], P(None, 'tp'), may hold values from -0.125 to 0.125
- up_weight: bfloat16 [2048, 6144], P(None, 'tp'), may hold values from -0.125 to 0.125
- down_weight: bfloat16 [6144, 2048], P('tp'), may hold values from -0.078125 to 0.078125
Outputs:
- new_hidden: bfloat16 [32, 104, 2048], P('seq', None, 'tp')
The draws below stay inside these ranges and needn't reach their ends.
Inputs may be any that keep to these rules, and one draw needn't show every extreme that they name: `selected_index`: each row holds 104 distinct positions in increasing order. `slot_spans`: each span of each request is held by exactly one slot. `span_order`: each row places the 8 spans of a request in some order.
All inputs are finite; a program needn't handle non-finite values.
Results may differ from the reference program's by a relative error of at most 0.027.
Values may be sent and summed in bfloat16 or wider, within the bound.
No kernel may reach another device: no remote copies, remote signals or barrier semaphores. Data moves between devices by JAX's collectives and lax.ppermute only.
A program may use at most 128 MiB of HBM per device.

```python
import math
import jax
import jax.numpy as jnp
from jax import lax

D = 2048
FF = 6144
QH = 16
KVH = 8
HD = 128
L = 1024
CH = 8
SEL_CH = 104
SLOTS = 32
REQ = 4


def draw_selected_index(key, part):
    slot_keys = jax.random.split(jax.random.fold_in(key, 3), SLOTS)

    def one_slot(slot_key):
        return jnp.sort(jax.random.permutation(slot_key, L)[:SEL_CH]).astype(jnp.int32)
    return jax.vmap(one_slot)(slot_keys)


def draw_cached_keys(key, part):
    values = jax.random.normal(jax.random.fold_in(key, 5), (SLOTS, L, KVH * HD), jnp.float32) * 1.5
    return jnp.clip(values, -48.0, 48.0).astype(jnp.bfloat16)


def place_ends(drawn, key, least, top_value):
    index_at = [jax.random.randint(jax.random.fold_in(key, axis), (), 0, length) for axis, length in enumerate(drawn.shape)]
    main_axis = drawn.shape.index(max(drawn.shape))
    beside = index_at[:main_axis] + [(index_at[main_axis] + 1) % drawn.shape[main_axis]] + index_at[main_axis + 1:]
    return drawn.at[tuple(index_at)].set(least).at[tuple(beside)].set(top_value)


def steps_of(key, extent, pieces, least, top_value):
    level, own = 1.0, jax.random.fold_in(key, 6)
    for axis_at, blocks in pieces:
        draws = jnp.exp(jax.random.uniform(jax.random.fold_in(own, axis_at), (blocks,), jnp.float32, least / len(pieces), top_value / len(pieces)))
        level = level * jnp.repeat(draws, extent[axis_at] // blocks).reshape([-1 if axis == axis_at else 1 for axis in range(len(extent))])
    return level


def scatter_about(own_key, extent, width, limit, cuts=(), kind=jnp.bfloat16):
    gain = steps_of(own_key, extent, cuts, -0.22, 0.18) if cuts else 1.0
    array = jax.random.normal(own_key, extent, jnp.float32) * width * gain
    return jnp.minimum(jnp.maximum(array, -limit), limit).astype(kind)


def setup_inputs(seed: int = 0) -> dict:
    key_of = jax.random.split(jax.random.key(seed), 19)
    selected_hidden = scatter_about(key_of[0], (SLOTS, SEL_CH, D), 1.0, 6.0, ((0, 16), (2, 8)))
    cached_keys = draw_cached_keys(jax.random.fold_in(key_of[18], 71), 0)
    cached_values = scatter_about(key_of[2], (SLOTS, L, KVH * HD), 1.0, 6.0, ((0, 16), (2, 8)))
    slot_spans = jax.random.permutation(key_of[3], SLOTS).astype(jnp.int32)
    span_order = jax.vmap(lambda own: jax.random.permutation(own, CH))(jax.random.split(key_of[4], REQ)).reshape((REQ, CH)).astype(jnp.int32)
    cache_start = place_ends(jax.random.randint(key_of[5], (REQ, CH), 0, 2 * CH * L), jax.random.fold_in(key_of[5], 1), 0, (2 * CH * L) - 1).astype(jnp.int32)
    selected_index = draw_selected_index(jax.random.fold_in(key_of[18], 71), 0)
    input_gain = jnp.clip(jnp.exp(jax.random.uniform(key_of[7], (D,), jnp.float32, math.log(0.5), math.log(2.0))), 0.5, 2.0).astype(jnp.bfloat16)
    query_weight = scatter_about(key_of[8], (D, QH * HD), D ** -0.5, 0.125, ((1, 8),))
    key_weight = scatter_about(key_of[9], (D, KVH * HD), D ** -0.5, 0.125, ((1, 8),))
    value_weight = scatter_about(key_of[10], (D, KVH * HD), D ** -0.5, 0.125, ((1, 8),))
    query_gain = jnp.clip(jnp.exp(jax.random.uniform(key_of[11], (HD,), jnp.float32, math.log(1.0), math.log(2.0))), 1.0, 2.0).astype(jnp.bfloat16)
    key_gain = jnp.clip(jnp.exp(jax.random.uniform(key_of[12], (HD,), jnp.float32, math.log(1.0), math.log(2.0))), 1.0, 2.0).astype(jnp.bfloat16)
    output_weight = scatter_about(key_of[13], (QH * HD, D), (QH * HD) ** -0.5, 0.125, ((0, 8),))
    post_gain = jnp.clip(jnp.exp(jax.random.uniform(key_of[14], (D,), jnp.float32, math.log(0.5), math.log(2.0))), 0.5, 2.0).astype(jnp.bfloat16)
    gate_weight = scatter_about(key_of[15], (D, FF), D ** -0.5, 0.125, ((1, 8),))
    up_weight = scatter_about(key_of[16], (D, FF), D ** -0.5, 0.125, ((1, 8),))
    down_weight = scatter_about(key_of[17], (FF, D), FF ** -0.5, 0.078125, ((0, 8),))
    return {"selected_hidden": selected_hidden, "cached_keys": cached_keys, "cached_values": cached_values, "slot_spans": slot_spans, "span_order": span_order, "cache_start": cache_start, "selected_index": selected_index, "input_gain": input_gain, "query_weight": query_weight, "key_weight": key_weight, "value_weight": value_weight, "query_gain": query_gain, "key_gain": key_gain, "output_weight": output_weight, "post_gain": post_gain, "gate_weight": gate_weight, "up_weight": up_weight, "down_weight": down_weight}


theta_base = 1000000.0
norm_eps = 1e-06

def rms_scale(values):
    return values * lax.rsqrt(lax.optimization_barrier(jnp.mean(values * values, axis=-1, keepdims=True)) + norm_eps)

def rotary(values, positions):
    half_len = values.shape[-1] // 2
    frequency = jnp.exp(-jnp.log(theta_base) * jnp.arange(half_len, dtype=jnp.float32) * 2.0 / values.shape[-1])
    angles = positions.astype(jnp.float32)[..., None] * frequency
    cosine = jnp.cos(angles)[..., None, :]
    sine_part = jnp.sin(angles)[..., None, :]
    lower_half = values[..., :half_len]
    upper_half = values[..., half_len:]
    return jnp.concatenate([lower_half * cosine - upper_half * sine_part, upper_half * cosine + lower_half * sine_part], axis=-1)

def reference(selected_hidden, cached_keys, cached_values, slot_spans, span_order, cache_start, selected_index, input_gain, query_weight, key_weight, value_weight, query_gain, key_gain, output_weight, post_gain, gate_weight, up_weight, down_weight):
    slot_request = slot_spans // CH
    slot_span = slot_spans % CH
    slot_base = span_order[slot_request, slot_span] * L
    slot_shift = slot_base - cache_start[slot_request, slot_span]
    row_count = SLOTS * SEL_CH
    hidden = selected_hidden.reshape(row_count, D)
    normed = (rms_scale(hidden.astype(jnp.float32)) * input_gain.astype(jnp.float32)).astype(jnp.bfloat16)
    query_pos = (slot_base[:, None] + selected_index).reshape(-1)
    query_proj = jnp.dot(normed, query_weight, preferred_element_type=jnp.float32).reshape(row_count, QH, HD)
    queries = rotary(rms_scale(query_proj) * query_gain.astype(jnp.float32), query_pos).astype(jnp.bfloat16)
    key_proj = jnp.dot(normed, key_weight, preferred_element_type=jnp.float32).reshape(row_count, KVH, HD)
    new_keys = rotary(rms_scale(key_proj) * key_gain.astype(jnp.float32), query_pos).astype(jnp.bfloat16)
    new_values = jnp.dot(normed, value_weight, preferred_element_type=jnp.float32).astype(jnp.bfloat16).reshape(row_count, KVH, HD)
    shift_pos = jnp.broadcast_to(slot_shift[:, None], (SLOTS, L))
    shifted = rotary(cached_keys.reshape(SLOTS, L, KVH, HD).astype(jnp.float32), shift_pos).astype(jnp.bfloat16)
    slot_rows = jnp.arange(SLOTS, dtype=jnp.int32)[:, None]
    joined_keys = shifted.at[slot_rows, selected_index].set(new_keys.reshape(SLOTS, SEL_CH, KVH, HD))
    joined_values = cached_values.reshape(SLOTS, L, KVH, HD).at[slot_rows, selected_index].set(new_values.reshape(SLOTS, SEL_CH, KVH, HD))
    slot_of_span = jnp.argsort(slot_spans).astype(jnp.int32)
    request_keys = joined_keys[slot_of_span].reshape(REQ, CH * L, KVH, HD)
    request_values = joined_values[slot_of_span].reshape(REQ, CH * L, KVH, HD)
    key_pos = (span_order[:, :, None] * L + jnp.arange(L, dtype=jnp.int32)[None, None, :]).reshape(REQ, CH * L)

    def attend_slot(slot_id):
        request = slot_request[slot_id]
        slot_queries = lax.dynamic_slice_in_dim(queries, slot_id * SEL_CH, SEL_CH, 0).astype(jnp.float32)
        positions = lax.dynamic_slice_in_dim(query_pos, slot_id * SEL_CH, SEL_CH, 0)
        keys_here = jnp.repeat(request_keys[request].astype(jnp.float32), QH // KVH, axis=1)
        values_here = jnp.repeat(request_values[request].astype(jnp.float32), QH // KVH, axis=1)
        scores = jnp.einsum('qhd,khd->hqk', slot_queries, keys_here) * HD ** (-0.5)
        key_mask = (key_pos[request][None, :] <= positions[:, None])[None]
        masked = jnp.where(key_mask, scores, -jnp.inf)
        row_max = lax.optimization_barrier(jnp.max(masked, axis=-1, keepdims=True))
        weights = jnp.where(key_mask, jnp.exp(masked - row_max), 0.0)
        total = lax.optimization_barrier(jnp.sum(weights, axis=-1))
        rounded = lax.optimization_barrier(weights.astype(jnp.bfloat16)).astype(jnp.float32)
        summed = jnp.einsum('hqk,khd->qhd', rounded, values_here)
        return (summed / jnp.transpose(total)[:, :, None]).astype(jnp.bfloat16)
    attended = lax.map(attend_slot, jnp.arange(SLOTS, dtype=jnp.int32)).reshape(row_count, QH * HD)
    out_proj = jnp.dot(attended, output_weight, preferred_element_type=jnp.float32)
    stream = (hidden.astype(jnp.float32) + out_proj).astype(jnp.bfloat16)
    normed_post = (rms_scale(stream.astype(jnp.float32)) * post_gain.astype(jnp.float32)).astype(jnp.bfloat16)
    gate_values = jnp.dot(normed_post, gate_weight, preferred_element_type=jnp.float32)
    up_values = jnp.dot(normed_post, up_weight, preferred_element_type=jnp.float32)
    active = (jax.nn.silu(gate_values) * up_values).astype(jnp.bfloat16)
    result = (stream.astype(jnp.float32) + jnp.dot(active, down_weight, preferred_element_type=jnp.float32)).astype(jnp.bfloat16)
    return result.reshape(SLOTS, SEL_CH, D)
```

```python
import functools

import jax
import jax.numpy as jnp
from jax import lax
from jax.experimental import pallas as pl
from jax.experimental.pallas import tpu as pltpu
from jax.sharding import Mesh
from jax.sharding import PartitionSpec as P

theta_base = 1000000.0
norm_eps = 1e-06
NEG = -1e30
FAR = 1e9
TP = ("z", "xhi")
SEQ = ("xlo", "yhi", "ylo", "core")
VMEM = pl.BlockSpec(memory_space=pltpu.VMEM)
SMEM = pl.BlockSpec(memory_space=pltpu.SMEM)
ANY = pl.BlockSpec(memory_space=pl.ANY)
F32 = jnp.float32
BF16 = jnp.bfloat16


def rotation_tables(positions, head_dim):
    half = head_dim // 2
    frequency = jnp.exp(-jnp.log(theta_base) * jnp.arange(half, dtype=F32) * 2.0 / head_dim)
    angles = positions.astype(F32)[..., None] * frequency
    cosine, sine = jnp.cos(angles), jnp.sin(angles)
    return jnp.concatenate([cosine, cosine], -1), jnp.concatenate([-sine, sine], -1)


def rotate(values, cosine, sine):
    return values * cosine + pltpu.roll(values, values.shape[-1] // 2, values.ndim - 1) * sine


def swap(x, axes, mask, size):
    return lax.ppermute(x, axes, [(i, i ^ mask) for i in range(size)])


def rotate_keys_kernel(k_ref, c_ref, s_ref, o_ref):
    o_ref[0] = rotate(k_ref[0].astype(F32), c_ref[0], s_ref[0]).astype(BF16)


def rotate_keys(keys, cosine, sine):
    slots, span, hd = keys.shape
    return pl.pallas_call(
        rotate_keys_kernel,
        grid=(slots,),
        in_specs=[
            pl.BlockSpec((1, span, hd), lambda i: (i, 0, 0)),
            pl.BlockSpec((1, 1, hd), lambda i: (i, 0, 0)),
            pl.BlockSpec((1, 1, hd), lambda i: (i, 0, 0)),
        ],
        out_specs=pl.BlockSpec((1, span, hd), lambda i: (i, 0, 0)),
        out_shape=jax.ShapeDtypeStruct(keys.shape, BF16),
        name="rotate_keys",
    )(keys, cosine, sine)


def scale_of(pieces, width):
    total = jnp.sum(pieces[0] * pieces[0], axis=-1, keepdims=True)
    for piece in pieces[1:]:
        total = total + jnp.sum(piece * piece, axis=-1, keepdims=True)
    return lax.rsqrt(total / width + norm_eps)


def head_norm(values):
    return values * lax.rsqrt(jnp.mean(values * values, axis=-1, keepdims=True) + norm_eps)


def project_kernel(n, me_ref, *refs):
    pieces = refs[:n]
    gain, wq, wk, wv, qg, kg, cos, sin, q_out, kv_out = refs[n:]
    me = me_ref[0]
    width = pieces[0].shape[1]
    hd = qg.shape[1]
    xs = [p[...].astype(F32) for p in pieces]
    scale = scale_of(xs, n * width)
    q = k = v = None
    for step in range(n):
        src = jnp.bitwise_xor(me, step)
        rows = pl.ds(pl.multiple_of(src * width, width), width)
        x = (xs[step] * scale * gain[pl.ds(src, 1), :]).astype(BF16)
        dq = jnp.dot(x, wq[rows, :], preferred_element_type=F32)
        dk = jnp.dot(x, wk[rows, :], preferred_element_type=F32)
        dv = jnp.dot(x, wv[rows, :], preferred_element_type=F32)
        q, k, v = (dq, dk, dv) if q is None else (q + dq, k + dk, v + dv)
    c, s = cos[...], sin[...]
    for h in range(q.shape[1] // hd):
        part = q[:, h * hd : (h + 1) * hd]
        q_out[:, h * hd : (h + 1) * hd] = rotate(head_norm(part) * qg[...], c, s).astype(BF16)
    kv_out[:, :hd] = rotate(head_norm(k) * kg[...], c, s).astype(BF16)
    kv_out[:, hd:] = v.astype(BF16)


def attend_kernel(count, ids, tab, kpos, tq, *refs):
    q_in, kv_in, k_in, v_in = refs[0:4], refs[4:8], refs[8:12], refs[12:16]
    outs = refs[16:20]
    keys, values, queries, run_m, run_l, run_acc, sems = refs[20:]
    hd = keys.shape[2]
    span = k_in[0].shape[1]
    slots = keys.shape[0]
    place_at = tab.shape[0] // 2
    xy, mk = ids[0], ids[1]
    copies = []
    for p in range(4):
        for which, (src, dst) in enumerate(((k_in[p], keys), (v_in[p], values))):
            copies.append(
                pltpu.make_async_copy(
                    src, dst.at[pl.ds(2 * p, 2), pl.ds(0, span), :], sems.at[which, p]
                )
            )
    for c in copies:
        c.start()
    pad = keys.shape[1] - span - count
    for p in range(4):
        for j in range(2):
            fresh = kv_in[p][j * count : (j + 1) * count, :]
            zero = jnp.zeros((pad, hd), BF16)
            keys[2 * p + j, span:, :] = jnp.concatenate([fresh[:, :hd], zero], 0)
            values[2 * p + j, span:, :] = jnp.concatenate([fresh[:, hd:], zero], 0)
            rows = q_in[p][j * count : (j + 1) * count, :]
            queries[2 * p + j] = jnp.concatenate([rows[:, :hd], rows[:, hd:]], 0)
    for c in copies:
        c.wait()
    factor = hd**-0.5

    def one_query(qi, _):
        q_nat = jnp.bitwise_xor(xy, qi // 2)
        q_slot = q_nat * 8 + mk * 2 + qi % 2
        q_req, q_place = tab[q_slot], tab[place_at + q_slot]
        run_m[...] = jnp.full(run_m.shape, NEG, F32)
        run_l[...] = jnp.zeros(run_l.shape, F32)
        run_acc[...] = jnp.zeros(run_acc.shape, F32)

        def one_key(ki, _):
            k_nat = jnp.bitwise_xor(mk, ki // 2) * 2 + ki % 2
            k_slot = xy * 8 + k_nat
            k_req, k_place = tab[k_slot], tab[place_at + k_slot]

            @pl.when(jnp.logical_and(k_req == q_req, k_place <= q_place))
            def _():
                limit = jnp.where(k_place < q_place, 65536.0, 0.0)
                bound = tq[q_nat * 2 + qi % 2] + limit
                scores = lax.dot_general(
                    queries[qi], keys[ki], (((1,), (1,)), ((), ())), preferred_element_type=F32
                )
                scores = jnp.where(kpos[pl.ds(k_nat, 1), :] <= bound, scores, NEG)
                old = run_m[...]
                new = jnp.maximum(old, jnp.max(scores, axis=-1, keepdims=True))
                shrink = jnp.exp((old - new) * factor)
                weights = jnp.exp((scores - new) * factor)
                run_m[...] = new
                run_l[...] = run_l[...] * shrink + jnp.sum(weights, axis=-1, keepdims=True)
                run_acc[...] = run_acc[...] * shrink + jnp.dot(
                    weights.astype(BF16), values[ki], preferred_element_type=F32
                )

            return 0

        lax.fori_loop(0, slots, one_key, 0)
        total = run_l[...]
        some = total > 0.0
        safe = jnp.where(some, total, 1.0)
        out = (run_acc[...] / safe).astype(BF16)
        lse = jnp.where(some, run_m[...] * factor + jnp.log(safe), NEG)
        high = lse.astype(BF16)
        rest = lse - high.astype(F32)
        mid = rest.astype(BF16)
        low = (rest - mid.astype(F32)).astype(BF16)
        lane = lax.broadcasted_iota(jnp.int32, out.shape, 1)
        stats = jnp.where(
            lane == 0,
            high.astype(F32),
            jnp.where(lane == 1, mid.astype(F32), jnp.where(lane == 2, low.astype(F32), 0.0)),
        ).astype(BF16)
        for p in range(4):

            @pl.when(qi // 2 == p)
            def _(p=p):
                outs[p][qi % 2] = jnp.concatenate([out, stats], axis=1)

        return 0

    lax.fori_loop(0, slots, one_query, 0)


def merge_kernel(n, count, me_ref, *refs):
    parts, wo, outs = refs[:4], refs[4], refs[5:]
    me = me_ref[0]
    hd = parts[0].shape[2] // 2
    width = outs[0].shape[1]
    rows = [[], []]
    for j in range(2):
        lses = []
        for part in parts:
            st = part[j, :, hd:].astype(F32)
            lses.append(st[:, 0:1] + st[:, 1:2] + st[:, 2:3])
        top = functools.reduce(jnp.maximum, lses)
        total = acc = None
        for lse, part in zip(lses, parts):
            w = jnp.exp(lse - top)
            term = w * part[j, :, :hd].astype(F32)
            total, acc = (w, term) if total is None else (total + w, acc + term)
        acc = acc / total
        for h in range(2):
            rows[h].append(acc[h * count : (h + 1) * count])
    att = jnp.concatenate([jnp.concatenate(r, 0) for r in rows], 1).astype(BF16)
    for step in range(n):
        src = jnp.bitwise_xor(me, step)
        cols = pl.ds(pl.multiple_of(src * width, width), width)
        outs[step][...] = jnp.dot(att, wo[:, cols], preferred_element_type=F32).astype(BF16)


def feed_kernel(n, me_ref, *refs):
    pieces = refs[:n]
    gain, wg, wu, wd = refs[n : n + 4]
    outs = refs[n + 4 :]
    me = me_ref[0]
    width = pieces[0].shape[1]
    xs = [p[...].astype(F32) for p in pieces]
    scale = scale_of(xs, n * width)
    g = u = None
    for step in range(n):
        src = jnp.bitwise_xor(me, step)
        rows = pl.ds(pl.multiple_of(src * width, width), width)
        x = (xs[step] * scale * gain[pl.ds(src, 1), :]).astype(BF16)
        dg = jnp.dot(x, wg[rows, :], preferred_element_type=F32)
        du = jnp.dot(x, wu[rows, :], preferred_element_type=F32)
        g, u = (dg, du) if g is None else (g + dg, u + du)
    active = (g / (1.0 + jnp.exp(-g)) * u).astype(BF16)
    for step in range(n):
        src = jnp.bitwise_xor(me, step)
        cols = pl.ds(pl.multiple_of(src * width, width), width)
        outs[step][...] = jnp.dot(active, wd[:, cols], preferred_element_type=F32).astype(BF16)


def on_device(
    selected_hidden,
    cached_keys,
    cached_values,
    slot_spans,
    span_order,
    cache_start,
    selected_index,
    input_gain,
    query_weight,
    key_weight,
    value_weight,
    query_gain,
    key_gain,
    output_weight,
    post_gain,
    gate_weight,
    up_weight,
    down_weight,
):
    slot_local, count, width = selected_hidden.shape
    span = cached_keys.shape[1]
    hd = query_gain.shape[0]
    rows = slot_local * count
    spans = span_order.shape[1]
    n = 8
    params = pltpu.CompilerParams(vmem_limit_bytes=48 << 20)

    def shaped(*shape, dtype=BF16):
        return jax.ShapeDtypeStruct(shape, dtype)

    xy = lax.axis_index(("xlo", "yhi"))
    mk = lax.axis_index(("ylo", "core"))
    me = lax.axis_index(TP).reshape(1)
    first_slot = lax.axis_index(SEQ) * slot_local

    hit = slot_spans[:, None] == jnp.arange(span_order.size, dtype=jnp.int32)[None, :]
    place = jnp.sum(jnp.where(hit, span_order.reshape(-1)[None, :], 0), axis=1)
    start = jnp.sum(jnp.where(hit, cache_start.reshape(-1)[None, :], 0), axis=1)
    table = jnp.concatenate([slot_spans // spans, place])
    ids = jnp.stack([xy, mk])
    base_here = lax.dynamic_slice_in_dim(place * span, first_slot, slot_local, 0)
    start_here = lax.dynamic_slice_in_dim(start, first_slot, slot_local, 0)
    index_here = lax.dynamic_slice_in_dim(selected_index, first_slot, slot_local, 0)

    hidden = selected_hidden.reshape(rows, width)
    pieces = [hidden] + [swap(hidden, TP, k, n) for k in range(1, n)]

    kc, ks = rotation_tables(base_here - start_here, hd)
    keys = rotate_keys(cached_keys, kc[:, None, :], ks[:, None, :])
    keys_y = swap(keys, "ylo", 1, 2)
    values_y = swap(cached_values, "ylo", 1, 2)
    key_set = [keys, swap(keys, "core", 1, 2), keys_y, swap(keys_y, "core", 1, 2)]
    value_set = [
        cached_values,
        swap(cached_values, "core", 1, 2),
        values_y,
        swap(values_y, "core", 1, 2),
    ]

    qc, qs = rotation_tables((base_here[:, None] + index_here).reshape(-1), hd)
    queries, fresh = pl.pallas_call(
        functools.partial(project_kernel, n),
        in_specs=[SMEM] + [VMEM] * (n + 8),
        out_specs=[VMEM, VMEM],
        out_shape=[shaped(rows, query_weight.shape[1]), shaped(rows, 2 * hd)],
        compiler_params=params,
        name="project",
    )(
        me,
        *pieces,
        input_gain.astype(F32).reshape(n, width),
        query_weight,
        key_weight,
        value_weight,
        query_gain.astype(F32)[None],
        key_gain.astype(F32)[None],
        qc,
        qs,
    )
    fresh_y = swap(fresh, "ylo", 1, 2)
    fresh_set = [fresh, swap(fresh, "core", 1, 2), fresh_y, swap(fresh_y, "core", 1, 2)]
    query_set = [queries] + [swap(queries, ("xlo", "yhi"), k, 4) for k in (1, 2, 3)]

    group_index = lax.dynamic_slice_in_dim(selected_index, xy * 8, 8, 0)
    token = jnp.arange(span, dtype=jnp.int32)
    taken = jnp.any(group_index[:, :, None] == token[None, None, :], axis=1)
    kpos = jnp.concatenate(
        [
            jnp.where(taken, FAR, token[None, :].astype(F32)),
            group_index.astype(F32),
            jnp.full((8, 128 - count), FAR, F32),
        ],
        axis=1,
    )
    query_index = lax.dynamic_slice_in_dim(
        selected_index.reshape(4, 4, slot_local, count), mk, 1, 1
    ).reshape(8, count)
    tq = jnp.concatenate([query_index, query_index], axis=1).astype(F32)[:, :, None]

    key_rows = span + 128
    parts = pl.pallas_call(
        functools.partial(attend_kernel, count),
        in_specs=[SMEM, SMEM, VMEM, VMEM] + [VMEM] * 8 + [ANY] * 8,
        out_specs=[VMEM] * 4,
        out_shape=[shaped(slot_local, 2 * count, 2 * hd)] * 4,
        scratch_shapes=[
            pltpu.VMEM((8, key_rows, hd), BF16),
            pltpu.VMEM((8, key_rows, hd), BF16),
            pltpu.VMEM((8, 2 * count, hd), BF16),
            pltpu.VMEM((2 * count, 1), F32),
            pltpu.VMEM((2 * count, 1), F32),
            pltpu.VMEM((2 * count, hd), F32),
            pltpu.SemaphoreType.DMA((2, 4)),
        ],
        compiler_params=params,
        name="attend",
    )(ids, table, kpos, tq, *query_set, *fresh_set, *key_set, *value_set)
    parts = [parts[0]] + [swap(parts[k], ("xlo", "yhi"), k, 4) for k in (1, 2, 3)]

    projected = pl.pallas_call(
        functools.partial(merge_kernel, n, count),
        in_specs=[SMEM] + [VMEM] * 5,
        out_specs=[VMEM] * n,
        out_shape=[shaped(rows, width)] * n,
        compiler_params=params,
        name="merge",
    )(me, *parts, output_weight)
    total = hidden.astype(F32) + projected[0].astype(F32)
    for k in range(1, n):
        total = total + swap(projected[k], TP, k, n).astype(F32)
    stream = total.astype(BF16)

    pieces = [stream] + [swap(stream, TP, k, n) for k in range(1, n)]
    downs = pl.pallas_call(
        functools.partial(feed_kernel, n),
        in_specs=[SMEM] + [VMEM] * (n + 4),
        out_specs=[VMEM] * n,
        out_shape=[shaped(rows, width)] * n,
        compiler_params=params,
        name="feed",
    )(
        me,
        *pieces,
        post_gain.astype(F32).reshape(n, width),
        gate_weight,
        up_weight,
        down_weight,
    )
    total = stream.astype(F32) + downs[0].astype(F32)
    for k in range(1, n):
        total = total + swap(downs[k], TP, k, n).astype(F32)
    return total.astype(BF16).reshape(slot_local, count, width)


def solution(mesh):
    fine = Mesh(
        mesh.devices.reshape(2, 2, 2, 2, 4, 2), ("xlo", "yhi", "ylo", "core", "z", "xhi")
    )
    in_specs = (
        P(SEQ, None, TP),
        P(SEQ, None, TP),
        P(SEQ, None, TP),
        P(),
        P(),
        P(),
        P(),
        P(),
        P(None, TP),
        P(None, TP),
        P(None, TP),
        P(),
        P(),
        P(TP, None),
        P(),
        P(None, TP),
        P(None, TP),
        P(TP, None),
    )
    return jax.shard_map(
        on_device, mesh=fine, in_specs=in_specs, out_specs=P(SEQ, None, TP), check_vma=False
    )
```

```python
import functools

import jax
import jax.numpy as jnp
from jax import lax
from jax.experimental import pallas as pl
from jax.experimental.pallas import tpu as pltpu
from jax.sharding import Mesh
from jax.sharding import PartitionSpec as P

theta_base = 1000000.0
norm_eps = 1e-06
NEG = -1e30
FAR = 1e9
TP = ("z", "xhi")
SEQ = ("xlo", "yhi", "ylo", "core")
ROUND = ("xlo", "yhi", "ylo")
FAR_MASKS = (3, 4, 7)
VMEM = pl.BlockSpec(memory_space=pltpu.VMEM)
SMEM = pl.BlockSpec(memory_space=pltpu.SMEM)
ANY = pl.BlockSpec(memory_space=pl.ANY)
F32 = jnp.float32
BF16 = jnp.bfloat16


def rotation_tables(positions, head_dim):
    half = head_dim // 2
    frequency = jnp.exp(-jnp.log(theta_base) * jnp.arange(half, dtype=F32) * 2.0 / head_dim)
    angles = positions.astype(F32)[..., None] * frequency
    cosine, sine = jnp.cos(angles), jnp.sin(angles)
    return jnp.concatenate([cosine, cosine], -1), jnp.concatenate([-sine, sine], -1)


def rotate(values, cosine, sine):
    return values * cosine + pltpu.roll(values, values.shape[-1] // 2, values.ndim - 1) * sine


def grant(mib):
    return pltpu.CompilerParams(vmem_limit_bytes=mib << 20)


def swap(x, axes, mask, size):
    return lax.ppermute(x, axes, [(i, i ^ mask) for i in range(size)])


def rotate_keys_kernel(k_ref, v_ref, c_ref, s_ref, o_ref):
    hd = k_ref.shape[2]
    o_ref[0, :, :hd] = rotate(k_ref[0].astype(F32), c_ref[0], s_ref[0]).astype(BF16)
    o_ref[0, :, hd:] = v_ref[0]


def rotate_keys(keys, values, cosine, sine):
    slots, span, hd = keys.shape
    return pl.pallas_call(
        rotate_keys_kernel,
        grid=(slots,),
        in_specs=[
            pl.BlockSpec((1, span, hd), lambda i: (i, 0, 0)),
            pl.BlockSpec((1, span, hd), lambda i: (i, 0, 0)),
            pl.BlockSpec((1, 1, hd), lambda i: (i, 0, 0)),
            pl.BlockSpec((1, 1, hd), lambda i: (i, 0, 0)),
        ],
        out_specs=pl.BlockSpec((1, span, 2 * hd), lambda i: (i, 0, 0)),
        out_shape=jax.ShapeDtypeStruct((slots, span, 2 * hd), BF16),
        compiler_params=grant(8),
        name="rotate_keys",
    )(keys, values, cosine, sine)


def scale_of(pieces, width):
    total = jnp.sum(pieces[0] * pieces[0], axis=-1, keepdims=True)
    for piece in pieces[1:]:
        total = total + jnp.sum(piece * piece, axis=-1, keepdims=True)
    return lax.rsqrt(total / width + norm_eps)


def head_norm(values):
    return values * lax.rsqrt(jnp.mean(values * values, axis=-1, keepdims=True) + norm_eps)


def project_kernel(n, me_ref, *refs):
    pairs = refs[: n // 2]
    gain, wq, wk, wv, qg, kg, cos, sin, q_out, kv_out = refs[n // 2 :]
    me = me_ref[0]
    width = pairs[0].shape[2]
    hd = qg.shape[1]
    xs = [p[i].astype(F32) for p in pairs for i in range(2)]
    scale = scale_of(xs, n * width)
    q = k = v = None
    for step in range(n):
        src = jnp.bitwise_xor(me, step)
        rows = pl.ds(pl.multiple_of(src * width, width), width)
        x = (xs[step] * scale * gain[pl.ds(src, 1), :]).astype(BF16)
        dq = jnp.dot(x, wq[rows, :], preferred_element_type=F32)
        dk = jnp.dot(x, wk[rows, :], preferred_element_type=F32)
        dv = jnp.dot(x, wv[rows, :], preferred_element_type=F32)
        q, k, v = (dq, dk, dv) if q is None else (q + dq, k + dk, v + dv)
    c, s = cos[...], sin[...]
    for h in range(q.shape[1] // hd):
        part = q[:, h * hd : (h + 1) * hd]
        q_out[:, h * hd : (h + 1) * hd] = rotate(head_norm(part) * qg[...], c, s).astype(BF16)
    kv_out[:, :hd] = rotate(head_norm(k) * kg[...], c, s).astype(BF16)
    kv_out[:, hd:] = v.astype(BF16)


def identity(rows, cols, period):
    row = lax.broadcasted_iota(jnp.int32, (rows, cols), 0)
    col = lax.broadcasted_iota(jnp.int32, (rows, cols), 1)
    return jnp.where(lax.rem(row, period) == col, 1.0, 0.0).astype(BF16)


def attend_kernel(count, ids, tab, kpos, q_index, *refs):
    q_in, kv_in, cached = refs[0:4], refs[4:8], refs[8:12]
    outs = refs[12:16]
    keys, values, queries, tq, run_m, run_l, run_acc, sems = refs[16:]
    hd = keys.shape[2]
    span = cached[0].shape[1]
    slots = keys.shape[0]
    place_at = tab.shape[0] // 2
    xy, mk = ids[0], ids[1]
    copies = []
    for p in range(4):
        for which, dst in enumerate((keys, values)):
            copies.append(
                pltpu.make_async_copy(
                    cached[p].at[:, :, pl.ds(which * hd, hd)],
                    dst.at[pl.ds(2 * p, 2), pl.ds(0, span), :],
                    sems.at[which, p],
                )
            )
    for c in copies:
        c.start()
    pad = keys.shape[1] - span - count
    for p in range(4):
        for j in range(2):
            fresh = kv_in[p][j * count : (j + 1) * count, :]
            zero = jnp.zeros((pad, hd), BF16)
            keys[2 * p + j, span:, :] = jnp.concatenate([fresh[:, :hd], zero], 0)
            values[2 * p + j, span:, :] = jnp.concatenate([fresh[:, hd:], zero], 0)
            rows = q_in[p][j * count : (j + 1) * count, :]
            queries[2 * p + j] = jnp.concatenate([rows[:, :hd], rows[:, hd:]], 0)
    index = q_index[...].astype(F32)
    upper = jnp.floor(index * 0.125)
    digits = jnp.concatenate([upper, index - 8.0 * upper], 0).astype(BF16)
    columns = lax.dot_general(
        identity(2 * count, count, count),
        digits,
        (((1,), (1,)), ((), ())),
        preferred_element_type=F32,
    )
    for q in range(slots):
        tq[q] = 8.0 * columns[:, q : q + 1] + columns[:, slots + q : slots + q + 1]
    turn = identity(2 * count, 2 * hd, 4 * count)
    for c in copies:
        c.wait()
    factor = hd**-0.5

    def one_query(qi, _):
        p = qi // 2
        q_nat = jnp.bitwise_xor(xy, p)
        q_mk = jnp.bitwise_xor(mk, (p % 2) * 2)
        q_slot = q_nat * 8 + q_mk * 2 + qi % 2
        q_req, q_place = tab[q_slot], tab[place_at + q_slot]
        run_m[...] = jnp.full(run_m.shape, NEG, F32)
        run_l[...] = jnp.zeros(run_l.shape, F32)
        run_acc[...] = jnp.zeros(run_acc.shape, F32)

        def one_key(ki, _):
            k_nat = jnp.bitwise_xor(mk, ki // 2) * 2 + ki % 2
            k_slot = xy * 8 + k_nat
            k_req, k_place = tab[k_slot], tab[place_at + k_slot]

            @pl.when(jnp.logical_and(k_req == q_req, k_place <= q_place))
            def _():
                limit = jnp.where(k_place < q_place, 65536.0, 0.0)
                bound = tq[qi] + limit
                scores = lax.dot_general(
                    queries[qi], keys[ki], (((1,), (1,)), ((), ())), preferred_element_type=F32
                )
                scores = jnp.where(kpos[pl.ds(k_nat, 1), :] <= bound, scores, NEG)
                old = run_m[...]
                new = jnp.maximum(old, jnp.max(scores, axis=-1, keepdims=True))
                shrink = jnp.exp((old - new) * factor)
                weights = jnp.exp((scores - new) * factor)
                run_m[...] = new
                run_l[...] = run_l[...] * shrink + jnp.sum(weights, axis=-1, keepdims=True)
                run_acc[...] = run_acc[...] * shrink + jnp.dot(
                    weights.astype(BF16), values[ki], preferred_element_type=F32
                )

            return 0

        lax.fori_loop(0, slots, one_key, 0)
        total = run_l[...]
        some = total > 0.0
        safe = jnp.where(some, total, 1.0)
        out = (run_acc[...] / safe).astype(BF16)
        lse = jnp.where(some, run_m[...] * factor + jnp.log(safe), NEG)
        high = lse.astype(BF16)
        rest = lse - high.astype(F32)
        mid = rest.astype(BF16)
        low = (rest - mid.astype(F32)).astype(BF16)
        lane = lax.broadcasted_iota(jnp.int32, out.shape, 1)
        stats = jnp.where(
            lane == 0,
            high.astype(F32),
            jnp.where(lane == 1, mid.astype(F32), jnp.where(lane == 2, low.astype(F32), 0.0)),
        ).astype(BF16)
        flat = lax.dot_general(
            stats, turn, (((0,), (0,)), ((), ())), preferred_element_type=F32
        )[:8].astype(BF16)
        for dest in range(4):

            @pl.when(p == dest)
            def _(dest=dest):
                outs[dest][qi % 2] = jnp.concatenate([out, flat[:, :hd], flat[:, hd:]], axis=0)

        return 0

    lax.fori_loop(0, slots, one_query, 0)


def merge_kernel(n, count, me_ref, *refs):
    parts, wo, outs = refs[:4], refs[4], refs[5:]
    me = me_ref[0]
    hd = parts[0].shape[2]
    width = outs[0].shape[1]
    turn = identity(2 * count, 2 * hd, 4 * count)
    rows = [[], []]
    for j in range(2):
        lses = []
        for part in parts:
            flat = part[j, 2 * count :, :]
            st = sum(
                lax.dot_general(
                    turn[:, i * hd : (i + 1) * hd],
                    flat,
                    (((1,), (1,)), ((), ())),
                    preferred_element_type=F32,
                )[:, 8 * i : 8 * i + 8]
                for i in range(2)
            )
            lses.append(st[:, 0:1] + st[:, 1:2] + st[:, 2:3])
        top = functools.reduce(jnp.maximum, lses)
        total = acc = None
        for lse, part in zip(lses, parts):
            w = jnp.exp(lse - top)
            term = w * part[j, : 2 * count, :].astype(F32)
            total, acc = (w, term) if total is None else (total + w, acc + term)
        acc = acc / total
        for h in range(2):
            rows[h].append(acc[h * count : (h + 1) * count])
    att = jnp.concatenate([jnp.concatenate(r, 0) for r in rows], 1).astype(BF16)
    for step in range(n):
        src = jnp.bitwise_xor(me, step)
        cols = pl.ds(pl.multiple_of(src * width, width), width)
        outs[step][...] = jnp.dot(att, wo[:, cols], preferred_element_type=F32).astype(BF16)


def feed_kernel(n, me_ref, *refs):
    pieces = refs[:n]
    gain, wg, wu, wd = refs[n : n + 4]
    outs = refs[n + 4 :]
    me = me_ref[0]
    width = pieces[0].shape[1]
    xs = [p[...].astype(F32) for p in pieces]
    scale = scale_of(xs, n * width)
    g = u = None
    for step in range(n):
        src = jnp.bitwise_xor(me, step)
        rows = pl.ds(pl.multiple_of(src * width, width), width)
        x = (xs[step] * scale * gain[pl.ds(src, 1), :]).astype(BF16)
        dg = jnp.dot(x, wg[rows, :], preferred_element_type=F32)
        du = jnp.dot(x, wu[rows, :], preferred_element_type=F32)
        g, u = (dg, du) if g is None else (g + dg, u + du)
    active = (g / (1.0 + jnp.exp(-g)) * u).astype(BF16)
    for step in range(n):
        src = jnp.bitwise_xor(me, step)
        cols = pl.ds(pl.multiple_of(src * width, width), width)
        outs[step][...] = jnp.dot(active, wd[:, cols], preferred_element_type=F32).astype(BF16)


def on_device(
    selected_hidden,
    cached_keys,
    cached_values,
    slot_spans,
    span_order,
    cache_start,
    selected_index,
    input_gain,
    query_weight,
    key_weight,
    value_weight,
    query_gain,
    key_gain,
    output_weight,
    post_gain,
    gate_weight,
    up_weight,
    down_weight,
):
    slot_local, count, width = selected_hidden.shape
    span = cached_keys.shape[1]
    hd = query_gain.shape[0]
    rows = slot_local * count
    spans = span_order.shape[1]
    n = 8

    def shaped(*shape, dtype=BF16):
        return jax.ShapeDtypeStruct(shape, dtype)

    xy = lax.axis_index(("xlo", "yhi"))
    mk = lax.axis_index(("ylo", "core"))
    me = lax.axis_index(TP).reshape(1)
    first_slot = lax.axis_index(SEQ) * slot_local

    number = lax.broadcasted_iota(jnp.int32, span_order.shape, 0) * spans
    number = number + lax.broadcasted_iota(jnp.int32, span_order.shape, 1)
    hit = slot_spans[:, None, None] == number[None]
    place = jnp.sum(jnp.where(hit, span_order[None], 0), axis=(1, 2))
    start = jnp.sum(jnp.where(hit, cache_start[None], 0), axis=(1, 2))
    table = jnp.concatenate([slot_spans // spans, place])
    ids = jnp.stack([xy, mk])
    base_here = lax.dynamic_slice_in_dim(place * span, first_slot, slot_local, 0)
    start_here = lax.dynamic_slice_in_dim(start, first_slot, slot_local, 0)

    hidden = selected_hidden.reshape(rows, width)
    pair = jnp.stack([hidden, swap(hidden, "xhi", 1, 2)])

    pair, selected_later, input_gain, post_gain = lax.optimization_barrier(
        (pair, selected_index, input_gain, post_gain)
    )
    pairs = [pair] + [swap(pair, "z", k, 4) for k in (1, 2, 3)]

    kc, ks = rotation_tables(base_here - start_here, hd)
    cached = rotate_keys(cached_keys, cached_values, kc[:, None, :], ks[:, None, :])
    cached_y = swap(cached, "ylo", 1, 2)

    index_here = lax.dynamic_slice_in_dim(selected_later, first_slot, slot_local, 0)
    qc, qs = rotation_tables((base_here[:, None] + index_here).reshape(-1), hd)
    group_index = lax.dynamic_slice_in_dim(selected_later, xy * 8, 8, 0)
    token = jnp.arange(span, dtype=jnp.int32)
    taken = jnp.any(group_index[:, :, None] == token[None, None, :], axis=1)
    kpos = jnp.concatenate(
        [
            jnp.where(taken, FAR, token[None, :].astype(F32)),
            group_index.astype(F32),
            jnp.full((8, 128 - count), FAR, F32),
        ],
        axis=1,
    )
    seq = lax.axis_index(SEQ)
    query_index = jnp.concatenate(
        [
            lax.dynamic_slice_in_dim(
                selected_later, jnp.bitwise_xor(seq, 2 * k) * slot_local, slot_local, 0
            )
            for k in (0,) + FAR_MASKS
        ],
        axis=0,
    )

    input_gain = input_gain.astype(F32).reshape(n, width)
    post_gain = post_gain.astype(F32).reshape(n, width)
    qg, kg = query_gain.astype(F32)[None], key_gain.astype(F32)[None]
    pairs[0], input_gain, post_gain, qg, kg, qc, qs, ids, table, kpos, query_index = (
        lax.optimization_barrier(
            (pairs[0], input_gain, post_gain, qg, kg, qc, qs, ids, table, kpos, query_index)
        )
    )
    queries, fresh = pl.pallas_call(
        functools.partial(project_kernel, n),
        in_specs=[SMEM] + [VMEM] * (n // 2 + 8),
        out_specs=[VMEM, VMEM],
        out_shape=[shaped(rows, query_weight.shape[1]), shaped(rows, 2 * hd)],
        compiler_params=grant(10),
        name="project",
    )(
        me,
        *pairs,
        input_gain,
        query_weight,
        key_weight,
        value_weight,
        qg,
        kg,
        qc,
        qs,
    )
    cached_y = lax.optimization_barrier((cached_y, fresh))[0]
    cached_set = [cached, swap(cached, "core", 1, 2), cached_y, swap(cached_y, "core", 1, 2)]
    fresh_y = swap(fresh, "ylo", 1, 2)
    fresh_set = [fresh, swap(fresh, "core", 1, 2), fresh_y, swap(fresh_y, "core", 1, 2)]
    query_set = [queries] + [swap(queries, ROUND, k, 8) for k in FAR_MASKS]

    key_rows = span + 128
    parts = pl.pallas_call(
        functools.partial(attend_kernel, count),
        in_specs=[SMEM, SMEM, VMEM, VMEM] + [VMEM] * 8 + [ANY] * 4,
        out_specs=[VMEM] * 4,
        out_shape=[shaped(slot_local, 2 * count + 16, hd)] * 4,
        scratch_shapes=[
            pltpu.VMEM((8, key_rows, hd), BF16),
            pltpu.VMEM((8, key_rows, hd), BF16),
            pltpu.VMEM((8, 2 * count, hd), BF16),
            pltpu.VMEM((8, 2 * count, 1), F32),
            pltpu.VMEM((2 * count, 1), F32),
            pltpu.VMEM((2 * count, 1), F32),
            pltpu.VMEM((2 * count, hd), F32),
            pltpu.SemaphoreType.DMA((2, 4)),
        ],
        compiler_params=grant(18),
        name="attend",
    )(ids, table, kpos, query_index, *query_set, *fresh_set, *cached_set)
    parts = [parts[0]] + [swap(part, ROUND, k, 8) for part, k in zip(parts[1:], FAR_MASKS)]

    projected = pl.pallas_call(
        functools.partial(merge_kernel, n, count),
        in_specs=[SMEM] + [VMEM] * 5,
        out_specs=[VMEM] * n,
        out_shape=[shaped(rows, width)] * n,
        compiler_params=grant(8),
        name="merge",
    )(me, *parts, output_weight)
    total = hidden.astype(F32) + projected[0].astype(F32)
    for k in range(1, n):
        total = total + swap(projected[k], TP, k, n).astype(F32)
    stream = total.astype(BF16)

    pieces = [stream] + [swap(stream, TP, k, n) for k in range(1, n)]
    downs = pl.pallas_call(
        functools.partial(feed_kernel, n),
        in_specs=[SMEM] + [VMEM] * (n + 4),
        out_specs=[VMEM] * n,
        out_shape=[shaped(rows, width)] * n,
        compiler_params=grant(18),
        name="feed",
    )(
        me,
        *pieces,
        post_gain,
        gate_weight,
        up_weight,
        down_weight,
    )
    total = stream.astype(F32) + downs[0].astype(F32)
    for k in range(1, n):
        total = total + swap(downs[k], TP, k, n).astype(F32)
    return total.astype(BF16).reshape(slot_local, count, width)


def solution(mesh):
    fine = Mesh(
        mesh.devices.reshape(2, 2, 2, 2, 4, 2), ("xlo", "yhi", "ylo", "core", "z", "xhi")
    )
    in_specs = (
        P(SEQ, None, TP),
        P(SEQ, None, TP),
        P(SEQ, None, TP),
        P(),
        P(),
        P(),
        P(),
        P(),
        P(None, TP),
        P(None, TP),
        P(None, TP),
        P(),
        P(),
        P(TP, None),
        P(),
        P(None, TP),
        P(None, TP),
        P(TP, None),
    )
    return jax.shard_map(
        on_device, mesh=fine, in_specs=in_specs, out_specs=P(SEQ, None, TP), check_vma=False
    )
```

```python
import functools
import math

import jax
import jax.numpy as jnp
from jax import lax
from jax.experimental import pallas as pl
from jax.experimental.pallas import tpu as pltpu
from jax.sharding import Mesh
from jax.sharding import PartitionSpec as P

theta_base = 1000000.0
norm_eps = 1e-06
NEG = -1e30
FAR = 1e9
TP = ("z", "xhi")
SEQ = ("xlo", "yhi", "ylo", "core")
ROUND = ("xlo", "yhi", "ylo")
FAR_MASKS = (3, 4, 7)
VMEM = pl.BlockSpec(memory_space=pltpu.VMEM)
SMEM = pl.BlockSpec(memory_space=pltpu.SMEM)
ANY = pl.BlockSpec(memory_space=pl.ANY)
HBM = pl.BlockSpec(memory_space=pltpu.HBM)
F32 = jnp.float32
BF16 = jnp.bfloat16


def rotation_tables(positions, head_dim):
    half = head_dim // 2
    frequency = jnp.exp(-jnp.log(theta_base) * jnp.arange(half, dtype=F32) * 2.0 / head_dim)
    angles = positions.astype(F32)[..., None] * frequency
    cosine, sine = jnp.cos(angles), jnp.sin(angles)
    return jnp.concatenate([cosine, cosine], -1), jnp.concatenate([-sine, sine], -1)


def rotate(values, cosine, sine):
    return values * cosine + pltpu.roll(values, values.shape[-1] // 2, values.ndim - 1) * sine


def grant(mib):
    return pltpu.CompilerParams(vmem_limit_bytes=mib << 20)


def swap(x, axes, mask, size):
    return lax.ppermute(x, axes, [(i, i ^ mask) for i in range(size)])


def scale_of(pieces, width):
    total = jnp.sum(pieces[0] * pieces[0], axis=-1, keepdims=True)
    for piece in pieces[1:]:
        total = total + jnp.sum(piece * piece, axis=-1, keepdims=True)
    return lax.rsqrt(total / width + norm_eps)


def head_norm(values):
    return values * lax.rsqrt(jnp.mean(values * values, axis=-1, keepdims=True) + norm_eps)


def project_kernel(n, me_ref, *refs):
    pairs = refs[: n // 2]
    gain, qg, kg, cos, sin = refs[n // 2 : n // 2 + 5]
    hbm, (q_out, kv_out) = refs[n // 2 + 5 : n // 2 + 8], refs[n // 2 + 8 : n // 2 + 10]
    (wq, wk, wv), sems = refs[n // 2 + 10 : -1], refs[-1]
    copies = [
        pltpu.make_async_copy(src, dst, sems.at[i])
        for i, (src, dst) in enumerate(zip(hbm, (wq, wk, wv)))
    ]
    for c in copies:
        c.start()
    me = me_ref[0]
    width = pairs[0].shape[2]
    hd = qg.shape[1]
    xs = [p[i].astype(F32) for p in pairs for i in range(2)]
    scale = scale_of(xs, n * width)
    for c in copies:
        c.wait()
    q = k = v = None
    for step in range(n):
        src = jnp.bitwise_xor(me, step)
        rows = pl.ds(pl.multiple_of(src * width, width), width)
        x = (xs[step] * scale * gain[rows].astype(F32)[None, :]).astype(BF16)
        dq = jnp.dot(x, wq[rows, :], preferred_element_type=F32)
        dk = jnp.dot(x, wk[rows, :], preferred_element_type=F32)
        dv = jnp.dot(x, wv[rows, :], preferred_element_type=F32)
        q, k, v = (dq, dk, dv) if q is None else (q + dq, k + dk, v + dv)
    c, s = cos[...], sin[...]
    for h in range(q.shape[1] // hd):
        part = q[:, h * hd : (h + 1) * hd]
        q_out[:, h * hd : (h + 1) * hd] = rotate(head_norm(part) * qg[...], c, s).astype(BF16)
    kv_out[:, :hd] = rotate(head_norm(k) * kg[...], c, s).astype(BF16)
    kv_out[:, hd:] = v.astype(BF16)


def identity(rows, cols, period):
    row = lax.broadcasted_iota(jnp.int32, (rows, cols), 0)
    col = lax.broadcasted_iota(jnp.int32, (rows, cols), 1)
    return jnp.where(lax.rem(row, period) == col, 1.0, 0.0).astype(BF16)


def attend_kernel(count, ids, tab, kpos, k_index, q_index, cos, sin, *refs):
    q_in, kv_in, cached = refs[0:4], refs[4:8], refs[8:12]
    outs = refs[12:16]
    keys, values, new_keys, queries, bounds, places, run_m, run_l, run_acc, todo, sems = refs[16:]
    hd = keys.shape[2]
    span = cached[0].shape[1]
    slots = keys.shape[0]
    place_at = tab.shape[0] // 2
    xy, mk = ids[0], ids[1]
    copies = []
    for p in range(4):
        for which, dst in enumerate((keys, values)):
            copies.append(
                pltpu.make_async_copy(
                    cached[p].at[pl.ds(2 * which, 2)],
                    dst.at[pl.ds(2 * p, 2), pl.ds(0, span), :],
                    sems.at[which, p],
                )
            )
    for c in copies:
        c.start()

    def scan_query(qi, n):
        p = qi // 2
        q_slot = jnp.bitwise_xor(xy, p) * 8 + jnp.bitwise_xor(mk, (p % 2) * 2) * 2 + qi % 2
        q_req, q_place = tab[q_slot], tab[place_at + q_slot]

        def scan_key(ki, n):
            k_nat = jnp.bitwise_xor(mk, ki // 2) * 2 + ki % 2
            k_slot = xy * 8 + k_nat
            k_req, k_place = tab[k_slot], tab[place_at + k_slot]
            seen = jnp.logical_and(k_req == q_req, k_place <= q_place)

            todo[0, n] = qi
            todo[1, n] = ki
            todo[2, n] = k_nat
            todo[3, n] = jnp.where(k_place < q_place, 65536, 0)
            return n + seen.astype(jnp.int32)

        return lax.fori_loop(0, slots, scan_key, n)

    found = lax.fori_loop(0, slots, scan_query, 0)
    todo[0, found] = 0
    todo[1, found] = 0
    todo[2, found] = 0
    todo[3, found] = -65536

    pad = values.shape[1] - span - count
    for p in range(4):
        for j in range(2):
            fresh = kv_in[p][j * count : (j + 1) * count, :]
            zero = jnp.zeros((pad, hd), BF16)
            new_keys[2 * p + j] = jnp.concatenate([fresh[:, :hd], zero], 0)
            values[2 * p + j, span:, :] = jnp.concatenate([fresh[:, hd:], zero], 0)
            rows = q_in[p][j * count : (j + 1) * count, :]
            queries[2 * p + j] = jnp.concatenate([rows[:, :hd], rows[:, hd:]], 0)
    places[:, :span] = kpos[...]
    places[:, span:] = jnp.concatenate(
        [k_index[...].astype(F32), jnp.full((slots, pad), FAR, F32)], axis=1
    )
    index = q_index[...].astype(F32)
    upper = jnp.floor(index * 0.125)
    digits = jnp.concatenate([upper, index - 8.0 * upper], 0).astype(BF16)
    columns = lax.dot_general(
        identity(2 * count, count, count),
        digits,
        (((1,), (1,)), ((), ())),
        preferred_element_type=F32,
    )
    for q in range(slots):
        bounds[q] = 8.0 * columns[:, q : q + 1] + columns[:, slots + q : slots + q + 1]
    run_m[...] = jnp.full(run_m.shape, NEG, F32)
    run_l[...] = jnp.zeros(run_l.shape, F32)
    run_acc[...] = jnp.zeros(run_acc.shape, F32)
    for c in copies:
        c.wait()
    factor = hd**-0.5 * math.log2(math.e)

    def score(at):
        qi, ki, row = todo[0, at], todo[1, at], pl.ds(todo[2, at], 1)
        query = queries[qi]
        turned = rotate(query.astype(F32), cos[row, :], sin[row, :]).astype(BF16)
        return jnp.concatenate(
            [
                lax.dot_general(
                    q, k[ki], (((1,), (1,)), ((), ())), preferred_element_type=F32
                )
                for q, k in ((turned, keys), (query, new_keys))
            ],
            axis=1,
        )

    def soften(at, scores):
        qi = todo[0, at]
        bound = bounds[qi] + todo[3, at].astype(F32)
        scores = jnp.where(places[pl.ds(todo[2, at], 1), :] <= bound, scores, NEG)
        old = run_m[qi]
        new = jnp.maximum(old, jnp.max(scores, axis=-1, keepdims=True))
        shrink = jnp.exp2((old - new) * factor)
        weights = jnp.exp2((scores - new) * factor)
        run_m[qi] = new
        run_l[qi] = run_l[qi] * shrink + jnp.sum(weights, axis=-1, keepdims=True)
        return shrink, weights.astype(BF16)

    def gather(at, shrink, weights):
        qi, ki = todo[0, at], todo[1, at]
        run_acc[qi] = run_acc[qi] * shrink + jnp.dot(
            weights, values[ki], preferred_element_type=F32
        )

    def two(i, _):
        first, second = 2 * i, 2 * i + 1
        s1 = score(first)
        s2 = score(second)
        soft1 = soften(first, s1)
        soft2 = soften(second, s2)
        gather(first, *soft1)
        gather(second, *soft2)
        return 0

    lax.fori_loop(0, (found + 1) // 2, two, 0)

    lane = lax.broadcasted_iota(jnp.int32, (2 * count, hd), 1)
    dest, entry, level = lane // 16, lane % 4, (lane % 16) // 4
    stats = jnp.zeros((2 * count, hd), F32)
    for p in range(4):
        for j in range(2):
            stats = jnp.where((dest == p) & (entry == j), run_m[2 * p + j], stats)
            stats = jnp.where((dest == p) & (entry == 2 + j), run_l[2 * p + j], stats)
    high = stats.astype(BF16).astype(F32)
    mid = (stats - high).astype(BF16).astype(F32)
    low = stats - high - mid
    stats = jnp.where(level == 0, high, jnp.where(level == 1, mid, low)).astype(BF16)
    flat = lax.dot_general(
        stats,
        identity(2 * count, 2 * hd, 4 * count),
        (((0,), (0,)), ((), ())),
        preferred_element_type=F32,
    ).astype(BF16)
    for p in range(4):
        for j in range(2):
            outs[p][j, : 2 * count, :] = run_acc[2 * p + j].astype(BF16)
            outs[p][j, 2 * count :, :] = flat[16 * p : 16 * p + 16, j * hd : (j + 1) * hd]


def attend(ids, table, kpos, key_index, query_index, cos, sin, queries, fresh, cached):
    count = query_index.shape[1]
    slot_local = cached[0].shape[0] // 2
    span, hd = cached[0].shape[1:]
    key_rows = span + 128
    return pl.pallas_call(
        functools.partial(attend_kernel, count),
        in_specs=[SMEM, SMEM] + [VMEM] * 13 + [ANY] * 4,
        out_specs=[VMEM] * 4,
        out_shape=[jax.ShapeDtypeStruct((slot_local, 2 * count + 16, hd), BF16)] * 4,
        scratch_shapes=[
            pltpu.VMEM((8, span, hd), BF16),
            pltpu.VMEM((8, key_rows, hd), BF16),
            pltpu.VMEM((8, key_rows - span, hd), BF16),
            pltpu.VMEM((8, 2 * count, hd), BF16),
            pltpu.VMEM((8, 2 * count, 1), F32),
            pltpu.VMEM((8, key_rows), F32),
            pltpu.VMEM((8, 2 * count, 1), F32),
            pltpu.VMEM((8, 2 * count, 1), F32),
            pltpu.VMEM((8, 2 * count, hd), F32),
            pltpu.SMEM((4, 72), jnp.int32),
            pltpu.SemaphoreType.DMA((2, 4)),
        ],
        compiler_params=grant(18),
        name="attend",
    )(ids, table, kpos, key_index, query_index, cos, sin, *queries, *fresh, *cached)


def merge_kernel(n, count, me_ref, *refs):
    parts, wo, outs = refs[:4], refs[4], refs[5:]
    me = me_ref[0]
    hd = parts[0].shape[2]
    width = outs[0].shape[1]
    turn = identity(2 * count, 2 * hd, 4 * count)
    tops, sums = [], []
    for part in parts:
        flat = jnp.concatenate([part[0, 2 * count :, :], part[1, 2 * count :, :]], axis=1)
        st = lax.dot_general(
            turn, flat, (((1,), (1,)), ((), ())), preferred_element_type=F32
        )
        st = st[:, 0:4] + st[:, 4:8] + st[:, 8:12]
        tops.append(st[:, 0:2])
        sums.append(st[:, 2:4])
    top = functools.reduce(jnp.maximum, tops)
    shares = [jnp.exp((m - top) * hd**-0.5) for m in tops]
    total = functools.reduce(jnp.add, [w * s for w, s in zip(shares, sums)])
    shares = [w / total for w in shares]
    rows = [[], []]
    for j in range(2):
        acc = functools.reduce(
            jnp.add,
            [
                w[:, j : j + 1] * part[j, : 2 * count, :].astype(F32)
                for w, part in zip(shares, parts)
            ],
        )
        for h in range(2):
            rows[h].append(acc[h * count : (h + 1) * count])
    att = jnp.concatenate([jnp.concatenate(r, 0) for r in rows], 1).astype(BF16)
    for step in range(n):
        src = jnp.bitwise_xor(me, step)
        cols = pl.ds(pl.multiple_of(src * width, width), width)
        outs[step][...] = jnp.dot(att, wo[:, cols], preferred_element_type=F32).astype(BF16)


def feed_kernel(n, me_ref, *refs):
    pieces = refs[:n]
    gain, wg, wu, wd = refs[n : n + 4]
    outs = refs[n + 4 :]
    me = me_ref[0]
    width = pieces[0].shape[1]
    xs = [p[...].astype(F32) for p in pieces]
    scale = scale_of(xs, n * width)
    g = u = None
    for step in range(n):
        src = jnp.bitwise_xor(me, step)
        rows = pl.ds(pl.multiple_of(src * width, width), width)
        x = (xs[step] * scale * gain[rows].astype(F32)[None, :]).astype(BF16)
        dg = jnp.dot(x, wg[rows, :], preferred_element_type=F32)
        du = jnp.dot(x, wu[rows, :], preferred_element_type=F32)
        g, u = (dg, du) if g is None else (g + dg, u + du)
    active = (g / (1.0 + jnp.exp(-g)) * u).astype(BF16)
    for step in range(n):
        src = jnp.bitwise_xor(me, step)
        cols = pl.ds(pl.multiple_of(src * width, width), width)
        outs[step][...] = jnp.dot(active, wd[:, cols], preferred_element_type=F32).astype(BF16)


def on_device(
    selected_hidden,
    cached_keys,
    cached_values,
    slot_spans,
    span_order,
    cache_start,
    selected_index,
    input_gain,
    query_weight,
    key_weight,
    value_weight,
    query_gain,
    key_gain,
    output_weight,
    post_gain,
    gate_weight,
    up_weight,
    down_weight,
):
    slot_local, count, width = selected_hidden.shape
    span = cached_keys.shape[1]
    hd = query_gain.shape[0]
    rows = slot_local * count
    spans = span_order.shape[1]
    n = 8

    def shaped(*shape, dtype=BF16):
        return jax.ShapeDtypeStruct(shape, dtype)

    xy = lax.axis_index(("xlo", "yhi"))
    mk = lax.axis_index(("ylo", "core"))
    me = lax.axis_index(TP).reshape(1)
    first_slot = lax.axis_index(SEQ) * slot_local

    number = lax.broadcasted_iota(jnp.int32, span_order.shape, 0) * spans
    number = number + lax.broadcasted_iota(jnp.int32, span_order.shape, 1)
    hit = slot_spans[:, None, None] == number[None]
    place = jnp.sum(jnp.where(hit, span_order[None], 0), axis=(1, 2))
    start = jnp.sum(jnp.where(hit, cache_start[None], 0), axis=(1, 2))
    table = jnp.concatenate([slot_spans // spans, place])
    ids = jnp.stack([xy, mk])
    base_here = lax.dynamic_slice_in_dim(place * span, first_slot, slot_local, 0)

    hidden = selected_hidden.reshape(rows, width)
    pair = jnp.stack([hidden, swap(hidden, "xhi", 1, 2)])

    pair, selected_later = lax.optimization_barrier((pair, selected_index))
    pairs = [pair] + [swap(pair, "z", k, 4) for k in (1, 2, 3)]

    cached = jnp.concatenate([cached_keys, cached_values], axis=0)
    cached_y = swap(cached, "ylo", 1, 2)
    cached_core = swap(cached, "core", 1, 2)

    index_here = lax.dynamic_slice_in_dim(selected_later, first_slot, slot_local, 0)
    qc, qs = rotation_tables(base_here[:, None] + index_here, hd)
    qc, qs = qc.reshape(rows, hd), qs.reshape(rows, hd)
    qg, kg = query_gain.astype(F32)[None], key_gain.astype(F32)[None]
    pairs[0], qg, kg, qc, qs, ids, table, cached_core = lax.optimization_barrier(
        (pairs[0], qg, kg, qc, qs, ids, table, cached_core)
    )
    queries, fresh = pl.pallas_call(
        functools.partial(project_kernel, n),
        in_specs=[SMEM] + [VMEM] * (n // 2 + 5) + [HBM] * 3,
        out_specs=[VMEM, VMEM],
        scratch_shapes=[
            pltpu.VMEM(w.shape, BF16) for w in (query_weight, key_weight, value_weight)
        ]
        + [pltpu.SemaphoreType.DMA((3,))],
        out_shape=[shaped(rows, query_weight.shape[1]), shaped(rows, 2 * hd)],
        compiler_params=grant(10),
        name="project",
    )(
        me,
        *pairs,
        input_gain,
        qg,
        kg,
        qc,
        qs,
        query_weight,
        key_weight,
        value_weight,
    )
    cached_y, selected_last, start, _ = lax.optimization_barrier(
        (cached_y, selected_later, start, fresh)
    )
    cached_set = [cached, cached_core, cached_y, swap(cached_y, "core", 1, 2)]
    fresh_y = swap(fresh, "ylo", 1, 2)
    fresh_set = [fresh, swap(fresh, "core", 1, 2), fresh_y, swap(fresh_y, "core", 1, 2)]
    query_set = [queries] + [swap(queries, ROUND, k, 8) for k in FAR_MASKS]

    group_index = lax.dynamic_slice_in_dim(selected_last, xy * 8, 8, 0)
    token = jnp.arange(span, dtype=jnp.int32)
    taken = jnp.any(group_index[:, :, None] == token[None, None, :], axis=1)
    kpos = jnp.where(taken, FAR, token[None, :].astype(F32))
    seq = lax.axis_index(SEQ)
    query_index = jnp.concatenate(
        [
            lax.dynamic_slice_in_dim(
                selected_last, jnp.bitwise_xor(seq, 2 * k) * slot_local, slot_local, 0
            )
            for k in (0,) + FAR_MASKS
        ],
        axis=0,
    )

    shift = lax.dynamic_slice_in_dim(place * span - start, xy * 8, 8, 0)
    kc, ks = rotation_tables(-shift, hd)
    parts = attend(
        ids,
        table,
        kpos,
        group_index,
        query_index,
        kc,
        ks,
        query_set,
        fresh_set,
        cached_set,
    )
    parts = [parts[0]] + [swap(part, ROUND, k, 8) for part, k in zip(parts[1:], FAR_MASKS)]

    projected = pl.pallas_call(
        functools.partial(merge_kernel, n, count),
        in_specs=[SMEM] + [VMEM] * 5,
        out_specs=[VMEM] * n,
        out_shape=[shaped(rows, width)] * n,
        compiler_params=grant(8),
        name="merge",
    )(me, *parts, output_weight)
    total = hidden.astype(F32) + projected[0].astype(F32)
    for k in range(1, n):
        total = total + swap(projected[k], TP, k, n).astype(F32)
    stream = total.astype(BF16)

    pieces = [stream] + [swap(stream, TP, k, n) for k in range(1, n)]
    downs = pl.pallas_call(
        functools.partial(feed_kernel, n),
        in_specs=[SMEM] + [VMEM] * (n + 4),
        out_specs=[VMEM] * n,
        out_shape=[shaped(rows, width)] * n,
        compiler_params=grant(18),
        name="feed",
    )(
        me,
        *pieces,
        post_gain,
        gate_weight,
        up_weight,
        down_weight,
    )
    total = stream.astype(F32) + downs[0].astype(F32)
    for k in range(1, n):
        total = total + swap(downs[k], TP, k, n).astype(F32)
    return total.astype(BF16).reshape(slot_local, count, width)


def solution(mesh):
    fine = Mesh(
        mesh.devices.reshape(2, 2, 2, 2, 4, 2), ("xlo", "yhi", "ylo", "core", "z", "xhi")
    )
    in_specs = (
        P(SEQ, None, TP),
        P(SEQ, None, TP),
        P(SEQ, None, TP),
        P(),
        P(),
        P(),
        P(),
        P(),
        P(None, TP),
        P(None, TP),
        P(None, TP),
        P(),
        P(),
        P(TP, None),
        P(),
        P(None, TP),
        P(None, TP),
        P(TP, None),
    )
    return jax.shard_map(
        on_device, mesh=fine, in_specs=in_specs, out_specs=P(SEQ, None, TP), check_vma=False
    )
```

```python
import functools
import math

import jax
import jax.numpy as jnp
from jax import lax
from jax.experimental import pallas as pl
from jax.experimental.pallas import tpu as pltpu
from jax.sharding import Mesh
from jax.sharding import PartitionSpec as P

theta_base = 1000000.0
norm_eps = 1e-06
NEG = -1e30
FAR = 1e9
TP = ("z", "xhi")
SEQ = ("xlo", "yhi", "ylo", "core")
ROUND = ("xlo", "yhi", "ylo")
FAR_MASKS = (3, 4, 7)
VMEM = pl.BlockSpec(memory_space=pltpu.VMEM)
SMEM = pl.BlockSpec(memory_space=pltpu.SMEM)
ANY = pl.BlockSpec(memory_space=pl.ANY)
HBM = pl.BlockSpec(memory_space=pltpu.HBM)
F32 = jnp.float32
BF16 = jnp.bfloat16


def rotation_tables(positions, head_dim):
    half = head_dim // 2
    frequency = jnp.exp(-jnp.log(theta_base) * jnp.arange(half, dtype=F32) * 2.0 / head_dim)
    angles = positions.astype(F32)[..., None] * frequency
    cosine, sine = jnp.cos(angles), jnp.sin(angles)
    return jnp.concatenate([cosine, cosine], -1), jnp.concatenate([-sine, sine], -1)


def rotate(values, cosine, sine):
    return values * cosine + pltpu.roll(values, values.shape[-1] // 2, values.ndim - 1) * sine


def grant(mib):
    return pltpu.CompilerParams(vmem_limit_bytes=mib << 20)


def swap(x, axes, mask, size):
    return lax.ppermute(x, axes, [(i, i ^ mask) for i in range(size)])


def cross(x, kind, flip):
    masks = {0: (0, 0), 1: (1, 3), 2: (3, 1), 3: (2, 2)}[kind]
    perm = []
    for core in range(2):
        for z in range(4):
            for hi in range(2):
                there = (core * 4 + (z ^ masks[core])) * 2 + (hi ^ flip)
                perm.append(((core * 4 + z) * 2 + hi, there))
    return lax.ppermute(x, ("core", "z", "xhi"), perm)


def scale_of(pieces, width):
    total = jnp.sum(pieces[0] * pieces[0], axis=-1, keepdims=True)
    for piece in pieces[1:]:
        total = total + jnp.sum(piece * piece, axis=-1, keepdims=True)
    return lax.rsqrt(total / width + norm_eps)


def head_norm(values):
    return values * lax.rsqrt(jnp.mean(values * values, axis=-1, keepdims=True) + norm_eps)


def project_kernel(n, me_ref, *refs):
    pairs = refs[: n // 2]
    gain, qg, kg, cos, sin = refs[n // 2 : n // 2 + 5]
    hbm, (q_out, kv_out) = refs[n // 2 + 5 : n // 2 + 8], refs[n // 2 + 8 : n // 2 + 10]
    (wq, wk, wv), sems = refs[n // 2 + 10 : -1], refs[-1]
    copies = [
        pltpu.make_async_copy(src, dst, sems.at[i])
        for i, (src, dst) in enumerate(zip(hbm, (wq, wk, wv)))
    ]
    for c in copies:
        c.start()
    me = me_ref[2]
    width = pairs[0].shape[2]
    hd = qg.shape[1]
    xs = [p[i].astype(F32) for p in pairs for i in range(2)]
    scale = scale_of(xs, n * width)
    for c in copies:
        c.wait()
    q = k = v = None
    for step in range(n):
        src = jnp.bitwise_xor(me, step)
        rows = pl.ds(pl.multiple_of(src * width, width), width)
        x = (xs[step] * scale * gain[rows].astype(F32)[None, :]).astype(BF16)
        dq = jnp.dot(x, wq[rows, :], preferred_element_type=F32)
        dk = jnp.dot(x, wk[rows, :], preferred_element_type=F32)
        dv = jnp.dot(x, wv[rows, :], preferred_element_type=F32)
        q, k, v = (dq, dk, dv) if q is None else (q + dq, k + dk, v + dv)
    c = cos[...].reshape(q.shape[0], hd)
    s = sin[...].reshape(q.shape[0], hd)
    for h in range(q.shape[1] // hd):
        part = q[:, h * hd : (h + 1) * hd]
        q_out[:, h * hd : (h + 1) * hd] = rotate(head_norm(part) * qg[...], c, s).astype(BF16)
    kv_out[:, :hd] = rotate(head_norm(k) * kg[...], c, s).astype(BF16)
    kv_out[:, hd:] = v.astype(BF16)


def identity(rows, cols, period):
    row = lax.broadcasted_iota(jnp.int32, (rows, cols), 0)
    col = lax.broadcasted_iota(jnp.int32, (rows, cols), 1)
    return jnp.where(lax.rem(row, period) == col, 1.0, 0.0).astype(BF16)


def attend_kernel(count, ids, tab, kpos, k_index, q_index, cos, sin, *refs):
    q_in, kv_in, cached = refs[0:4], refs[4:8], refs[8:12]
    outs = refs[12:16]
    keys, values, new_keys, queries, bounds, places, run_m, run_l, run_acc, todo, sems = refs[16:]
    hd = keys.shape[2]
    span = cached[0].shape[1]
    slots = keys.shape[0]
    place_at = tab.shape[0] // 2
    xy, mk = ids[0], ids[1]
    copies = []
    for p in range(4):
        for which, dst in enumerate((keys, values)):
            copies.append(
                pltpu.make_async_copy(
                    cached[p].at[pl.ds(2 * which, 2)],
                    dst.at[pl.ds(2 * p, 2), pl.ds(0, span), :],
                    sems.at[which, p],
                )
            )
    for c in copies:
        c.start()

    def scan_query(qi, n):
        p = qi // 2
        q_slot = jnp.bitwise_xor(xy, p) * 8 + jnp.bitwise_xor(mk, (p % 2) * 2) * 2 + qi % 2
        q_req, q_place = tab[q_slot], tab[place_at + q_slot]

        def scan_key(ki, n):
            k_nat = jnp.bitwise_xor(mk, ki // 2) * 2 + ki % 2
            k_slot = xy * 8 + k_nat
            k_req, k_place = tab[k_slot], tab[place_at + k_slot]
            seen = jnp.logical_and(k_req == q_req, k_place <= q_place)

            todo[0, n] = qi
            todo[1, n] = ki
            todo[2, n] = k_nat
            todo[3, n] = jnp.where(k_place < q_place, 65536, 0)
            return n + seen.astype(jnp.int32)

        return lax.fori_loop(0, slots, scan_key, n)

    found = lax.fori_loop(0, slots, scan_query, 0)
    todo[0, found] = 0
    todo[1, found] = 0
    todo[2, found] = 0
    todo[3, found] = -65536

    pad = values.shape[1] - span - count
    for p in range(4):
        for j in range(2):
            fresh = kv_in[p][j * count : (j + 1) * count, :]
            zero = jnp.zeros((pad, hd), BF16)
            new_keys[2 * p + j] = jnp.concatenate([fresh[:, :hd], zero], 0)
            values[2 * p + j, span:, :] = jnp.concatenate([fresh[:, hd:], zero], 0)
            rows = q_in[p][j * count : (j + 1) * count, :]
            queries[2 * p + j] = jnp.concatenate([rows[:, :hd], rows[:, hd:]], 0)
    places[:, :span] = kpos[...]
    places[:, span:] = jnp.concatenate(
        [k_index[...].astype(F32), jnp.full((slots, pad), FAR, F32)], axis=1
    )
    index = q_index[...].astype(F32)
    upper = jnp.floor(index * 0.125)
    digits = jnp.concatenate([upper, index - 8.0 * upper], 0).astype(BF16)
    columns = lax.dot_general(
        identity(2 * count, count, count),
        digits,
        (((1,), (1,)), ((), ())),
        preferred_element_type=F32,
    )
    for q in range(slots):
        bounds[q] = 8.0 * columns[:, q : q + 1] + columns[:, slots + q : slots + q + 1]
    run_m[...] = jnp.full(run_m.shape, NEG, F32)
    run_l[...] = jnp.zeros(run_l.shape, F32)
    run_acc[...] = jnp.zeros(run_acc.shape, F32)
    for c in copies:
        c.wait()
    factor = hd**-0.5 * math.log2(math.e)

    def score(at):
        qi, ki, row = todo[0, at], todo[1, at], pl.ds(todo[2, at], 1)
        query = queries[qi]
        turned = rotate(query.astype(F32), cos[row, :], sin[row, :]).astype(BF16)
        return jnp.concatenate(
            [
                lax.dot_general(
                    q, k[ki], (((1,), (1,)), ((), ())), preferred_element_type=F32
                )
                for q, k in ((turned, keys), (query, new_keys))
            ],
            axis=1,
        )

    def soften(at, scores):
        qi = todo[0, at]
        bound = bounds[qi] + todo[3, at].astype(F32)
        scores = jnp.where(places[pl.ds(todo[2, at], 1), :] <= bound, scores, NEG)
        old = run_m[qi]
        new = jnp.maximum(old, jnp.max(scores, axis=-1, keepdims=True))
        shrink = jnp.exp2((old - new) * factor)
        weights = jnp.exp2((scores - new) * factor)
        run_m[qi] = new
        run_l[qi] = run_l[qi] * shrink + jnp.sum(weights, axis=-1, keepdims=True)
        return shrink, weights.astype(BF16)

    def gather(at, shrink, weights):
        qi, ki = todo[0, at], todo[1, at]
        run_acc[qi] = run_acc[qi] * shrink + jnp.dot(
            weights, values[ki], preferred_element_type=F32
        )

    def two(i, _):
        first, second = 2 * i, 2 * i + 1
        s1 = score(first)
        s2 = score(second)
        soft1 = soften(first, s1)
        soft2 = soften(second, s2)
        gather(first, *soft1)
        gather(second, *soft2)
        return 0

    lax.fori_loop(0, (found + 1) // 2, two, 0)

    lane = lax.broadcasted_iota(jnp.int32, (2 * count, hd), 1)
    dest, entry, level = lane // 16, lane % 4, (lane % 16) // 4
    stats = jnp.zeros((2 * count, hd), F32)
    for p in range(4):
        for j in range(2):
            stats = jnp.where((dest == p) & (entry == j), run_m[2 * p + j], stats)
            stats = jnp.where((dest == p) & (entry == 2 + j), run_l[2 * p + j], stats)
    high = stats.astype(BF16).astype(F32)
    mid = (stats - high).astype(BF16).astype(F32)
    low = stats - high - mid
    stats = jnp.where(level == 0, high, jnp.where(level == 1, mid, low)).astype(BF16)
    flat = lax.dot_general(
        stats,
        identity(2 * count, 2 * hd, 4 * count),
        (((0,), (0,)), ((), ())),
        preferred_element_type=F32,
    ).astype(BF16)
    for p in range(4):
        for j in range(2):
            outs[p][j, : 2 * count, :] = run_acc[2 * p + j].astype(BF16)
            outs[p][j, 2 * count :, :] = flat[16 * p : 16 * p + 16, j * hd : (j + 1) * hd]


def attend(ids, table, kpos, key_index, query_index, cos, sin, queries, fresh, cached):
    count = query_index.shape[1]
    slot_local = cached[0].shape[0] // 2
    span, hd = cached[0].shape[1:]
    key_rows = span + 128
    return pl.pallas_call(
        functools.partial(attend_kernel, count),
        in_specs=[SMEM, SMEM] + [VMEM] * 13 + [ANY] * 4,
        out_specs=[VMEM] * 4,
        out_shape=[jax.ShapeDtypeStruct((slot_local, 2 * count + 16, hd), BF16)] * 4,
        scratch_shapes=[
            pltpu.VMEM((8, span, hd), BF16),
            pltpu.VMEM((8, key_rows, hd), BF16),
            pltpu.VMEM((8, key_rows - span, hd), BF16),
            pltpu.VMEM((8, 2 * count, hd), BF16),
            pltpu.VMEM((8, 2 * count, 1), F32),
            pltpu.VMEM((8, key_rows), F32),
            pltpu.VMEM((8, 2 * count, 1), F32),
            pltpu.VMEM((8, 2 * count, 1), F32),
            pltpu.VMEM((8, 2 * count, hd), F32),
            pltpu.SMEM((4, 72), jnp.int32),
            pltpu.SemaphoreType.DMA((2, 4)),
        ],
        compiler_params=grant(18),
        name="attend",
    )(ids, table, kpos, key_index, query_index, cos, sin, *queries, *fresh, *cached)


def merge_kernel(count, *refs):
    parts, out = refs[:4], refs[4]
    hd = parts[0].shape[2]
    turn = identity(2 * count, 2 * hd, 4 * count)
    tops, sums = [], []
    for part in parts:
        flat = jnp.concatenate([part[0, 2 * count :, :], part[1, 2 * count :, :]], axis=1)
        st = lax.dot_general(
            turn, flat, (((1,), (1,)), ((), ())), preferred_element_type=F32
        )
        st = st[:, 0:4] + st[:, 4:8] + st[:, 8:12]
        tops.append(st[:, 0:2])
        sums.append(st[:, 2:4])
    top = functools.reduce(jnp.maximum, tops)
    shares = [jnp.exp((m - top) * hd**-0.5) for m in tops]
    total = functools.reduce(jnp.add, [w * s for w, s in zip(shares, sums)])
    shares = [w / total for w in shares]
    rows = [[], []]
    for j in range(2):
        acc = functools.reduce(
            jnp.add,
            [
                w[:, j : j + 1] * part[j, : 2 * count, :].astype(F32)
                for w, part in zip(shares, parts)
            ],
        )
        for h in range(2):
            rows[h].append(acc[h * count : (h + 1) * count])
    out[...] = jnp.concatenate([jnp.concatenate(r, 0) for r in rows], 1).astype(BF16)


def feed_kernel(n, ids, *refs):
    pieces, pairs = refs[:n], refs[n : n + n // 2]
    wo_own = refs[n + n // 2 : 2 * n]
    wo_sibling = refs[2 * n : 2 * n + n // 2]
    gain, wg, wu, wd = refs[2 * n + n // 2 : 2 * n + n // 2 + 4]
    outs, mine = refs[2 * n + n // 2 + 4 : -2], refs[-2]
    stream = refs[-1]
    me, core = ids[2], ids[3]
    width = pieces[0].shape[1]
    half = width // 2
    total = None
    for weights, which in ((wo_own, core), (wo_sibling, 1 - core)):
        cols = pl.ds(pl.multiple_of(which * half, half), half)
        for i, weight in enumerate(weights):
            x = jnp.concatenate([pieces[2 * i][:, cols], pieces[2 * i + 1][:, cols]], axis=1)
            part = jnp.dot(x, weight[...], preferred_element_type=F32)
            total = part if total is None else total + part
    stream[...] = total
    for step in range(n):
        src = jnp.bitwise_xor(me, step)
        cols = pl.ds(pl.multiple_of(src * width, width), width)
        stream[:, cols] = stream[:, cols] + pairs[step // 2][step % 2].astype(F32)
        if step == 0:
            mine[...] = stream[:, cols].astype(BF16)
    xs = stream[...].astype(BF16).astype(F32)
    scale = scale_of([xs], n * width)
    x = (xs * scale * gain[...].astype(F32)[None, :]).astype(BF16)
    g = jnp.dot(x, wg[...], preferred_element_type=F32)
    u = jnp.dot(x, wu[...], preferred_element_type=F32)
    active = (g / (1.0 + jnp.exp(-g)) * u).astype(BF16)
    for step in range(n):
        src = jnp.bitwise_xor(me, step)
        cols = pl.ds(pl.multiple_of(src * width, width), width)
        outs[step][...] = jnp.dot(active, wd[:, cols], preferred_element_type=F32).astype(BF16)


def on_device(
    selected_hidden,
    cached_keys,
    cached_values,
    slot_spans,
    span_order,
    cache_start,
    selected_index,
    input_gain,
    query_weight,
    key_weight,
    value_weight,
    query_gain,
    key_gain,
    output_weight,
    post_gain,
    gate_weight,
    up_weight,
    down_weight,
):
    slot_local, count, width = selected_hidden.shape
    span = cached_keys.shape[1]
    hd = query_gain.shape[0]
    rows = slot_local * count
    spans = span_order.shape[1]
    n = 8

    def shaped(*shape, dtype=BF16):
        return jax.ShapeDtypeStruct(shape, dtype)

    def rows_at(array, start, size):
        return lax.dynamic_slice(array, (start, 0), (size, array.shape[1]), allow_negative_indices=False)

    hidden = selected_hidden.reshape(rows, width)
    half = output_weight.shape[0] // 2
    xy = lax.axis_index(("xlo", "yhi"))
    core = lax.axis_index("core")
    seq = lax.axis_index(SEQ)
    ids = jnp.stack([xy, lax.axis_index(("ylo", "core")), lax.axis_index(TP), core])

    number = lax.broadcasted_iota(jnp.int32, span_order.shape, 0) * spans
    number = number + lax.broadcasted_iota(jnp.int32, span_order.shape, 1)
    hit = slot_spans[:, None, None] == number[None]
    place = jnp.sum(jnp.where(hit, span_order[None], 0), axis=(1, 2))
    start = jnp.sum(jnp.where(hit, cache_start[None], 0), axis=(1, 2))
    table = jnp.concatenate([slot_spans // spans, place])

    pair = jnp.stack([hidden, swap(hidden, "xhi", 1, 2)])

    output_half = rows_at(output_weight, core * half, half)
    pair, selected_later, place, start, ids, at_group, *at_slots = lax.optimization_barrier(
        (pair, selected_index, place, start, ids, xy * 8)
        + tuple(jnp.bitwise_xor(seq, 2 * k) * slot_local for k in (0,) + FAR_MASKS)
    )
    output_x = swap(output_half, "xhi", 1, 2)
    pairs = [pair] + [swap(pair, "z", k, 4) for k in (1, 2, 3)]

    cached = jnp.concatenate([cached_keys, cached_values], axis=0)
    cached_y = swap(cached, "ylo", 1, 2)
    cached_core = swap(cached, "core", 1, 2)

    base_here = rows_at((place * span)[:, None], at_slots[0], slot_local)
    index_here = rows_at(selected_later, at_slots[0], slot_local)
    qc, qs = rotation_tables(base_here + index_here, hd)
    qg, kg = query_gain.astype(F32)[None], key_gain.astype(F32)[None]
    output_half, output_x, pairs[1] = lax.optimization_barrier(
        (output_half, output_x, pairs[1])
    )
    wo_0 = jnp.concatenate([output_half, output_x], axis=0)
    wo_1 = cross(wo_0, 1, 0)
    pairs[0], qg, kg, qc, qs, ids, table, cached_core = lax.optimization_barrier(
        (pairs[0], qg, kg, qc, qs, ids, table, cached_core)
    )
    queries, fresh = pl.pallas_call(
        functools.partial(project_kernel, n),
        in_specs=[SMEM] + [VMEM] * (n // 2 + 5) + [HBM] * 3,
        out_specs=[VMEM, VMEM],
        scratch_shapes=[
            pltpu.VMEM(w.shape, BF16) for w in (query_weight, key_weight, value_weight)
        ]
        + [pltpu.SemaphoreType.DMA((3,))],
        out_shape=[shaped(rows, query_weight.shape[1]), shaped(rows, 2 * hd)],
        compiler_params=grant(10),
        name="project",
    )(
        ids,
        *pairs,
        input_gain,
        qg,
        kg,
        qc,
        qs,
        query_weight,
        key_weight,
        value_weight,
    )
    cached_y, selected_last, start, _ = lax.optimization_barrier(
        (cached_y, selected_later, start, fresh)
    )
    cached_set = [cached, cached_core, cached_y, swap(cached_y, "core", 1, 2)]
    fresh_y = swap(fresh, "ylo", 1, 2)
    fresh_set = [fresh, swap(fresh, "core", 1, 2), fresh_y, swap(fresh_y, "core", 1, 2)]
    query_set = [queries] + [swap(queries, ROUND, k, 8) for k in FAR_MASKS]

    group_index = rows_at(selected_last, at_group, 8)
    token = jnp.arange(span, dtype=jnp.int32)
    taken = jnp.any(group_index[:, :, None] == token[None, None, :], axis=1)
    kpos = jnp.where(taken, FAR, token[None, :].astype(F32))
    query_index = jnp.concatenate(
        [rows_at(selected_last, at, slot_local) for at in at_slots], axis=0
    )
    query_set[1], wo_1 = lax.optimization_barrier((query_set[1], wo_1))
    wo_2 = cross(wo_0, 2, 0)
    wo_3 = cross(wo_1, 2, 0)
    wo_0, wo_1, query_set[3] = lax.optimization_barrier((wo_0, wo_1, query_set[3]))
    wo_0c, wo_1c = swap(wo_0, "core", 1, 2), swap(wo_1, "core", 1, 2)

    shift = rows_at((place * span - start)[:, None], at_group, 8)[:, 0]
    kc, ks = rotation_tables(-shift, hd)
    parts = attend(
        ids,
        table,
        kpos,
        group_index,
        query_index,
        kc,
        ks,
        query_set,
        fresh_set,
        cached_set,
    )
    *parts, wo_0c, wo_1c = lax.optimization_barrier((*parts, wo_0c, wo_1c))
    parts = [parts[0]] + [swap(part, ROUND, k, 8) for part, k in zip(parts[1:], FAR_MASKS)]

    attended = pl.pallas_call(
        functools.partial(merge_kernel, count),
        in_specs=[VMEM] * 4,
        out_specs=VMEM,
        out_shape=shaped(rows, width),
        compiler_params=grant(8),
        name="merge",
    )(*parts)
    order = [(kind, flip) for kind in range(4) for flip in range(2)]
    wo_2, wo_3, attended = lax.optimization_barrier((wo_2, wo_3, attended))
    wo_2c, wo_3c = swap(wo_2, "core", 1, 2), swap(wo_3, "core", 1, 2)
    wo_own = [wo_0, wo_1, wo_2, wo_3]
    wo_2c, wo_3c, later = lax.optimization_barrier((wo_2c, wo_3c, attended))
    pieces = [attended] + [
        cross(attended if i < 3 else later, kind, flip)
        for i, (kind, flip) in enumerate(order[1:])
    ]
    *downs, stream = pl.pallas_call(
        functools.partial(feed_kernel, n),
        in_specs=[SMEM] + [VMEM] * (2 * n + n // 2 + 4),
        out_specs=[VMEM] * (n + 1),
        out_shape=[shaped(rows, width)] * (n + 1),
        scratch_shapes=[pltpu.VMEM((rows, n * width), F32)],
        compiler_params=grant(20),
        name="feed",
    )(
        ids,
        *pieces,
        *pairs,
        *wo_own,
        wo_0c,
        wo_2c,
        wo_1c,
        wo_3c,
        post_gain,
        gate_weight,
        up_weight,
        down_weight,
    )
    total = stream.astype(F32) + downs[0].astype(F32)
    for k in range(1, n):
        total = total + swap(downs[k], TP, k, n).astype(F32)
    return total.astype(BF16).reshape(slot_local, count, width)


def solution(mesh):
    fine = Mesh(
        mesh.devices.reshape(2, 2, 2, 2, 4, 2), ("xlo", "yhi", "ylo", "core", "z", "xhi")
    )
    in_specs = (
        P(SEQ, None, TP),
        P(SEQ, None, TP),
        P(SEQ, None, TP),
        P(),
        P(),
        P(),
        P(),
        P(),
        P(None, TP),
        P(None, TP),
        P(None, TP),
        P(),
        P(),
        P(TP, None),
        P(),
        P(None, TP),
        P(None, TP),
        P(TP, None),
    )
    return jax.shard_map(
        on_device, mesh=fine, in_specs=in_specs, out_specs=P(SEQ, None, TP), check_vma=False
    )
```

```python
import functools
import math

import jax
import jax.numpy as jnp
from jax import lax
from jax.experimental import pallas as pl
from jax.experimental.pallas import tpu as pltpu
from jax.sharding import Mesh
from jax.sharding import PartitionSpec as P

theta_base = 1000000.0
norm_eps = 1e-06
NEG = -1e30
FAR = 1e9
TP = ("z", "xhi")
SEQ = ("xlo", "yhi", "ylo", "core")
ROUND = ("xlo", "yhi", "ylo")
FAR_MASKS = (3, 4, 7)
VMEM = pl.BlockSpec(memory_space=pltpu.VMEM)
SMEM = pl.BlockSpec(memory_space=pltpu.SMEM)
ANY = pl.BlockSpec(memory_space=pl.ANY)
HBM = pl.BlockSpec(memory_space=pltpu.HBM)
F32 = jnp.float32
BF16 = jnp.bfloat16


def rotation_tables(positions, head_dim):
    half = head_dim // 2
    frequency = jnp.exp(-jnp.log(theta_base) * jnp.arange(half, dtype=F32) * 2.0 / head_dim)
    angles = positions.astype(F32)[..., None] * frequency
    cosine, sine = jnp.cos(angles), jnp.sin(angles)
    return jnp.concatenate([cosine, cosine], -1), jnp.concatenate([-sine, sine], -1)


def rotate(values, cosine, sine):
    return values * cosine + pltpu.roll(values, values.shape[-1] // 2, values.ndim - 1) * sine


def grant(mib):
    return pltpu.CompilerParams(vmem_limit_bytes=mib << 20)


def swap(x, axes, mask, size):
    return lax.ppermute(x, axes, [(i, i ^ mask) for i in range(size)])


def cross(x, kind, flip):
    masks = {0: (0, 0), 1: (1, 3), 2: (3, 1), 3: (2, 2)}[kind]
    perm = []
    for core in range(2):
        for z in range(4):
            for hi in range(2):
                there = (core * 4 + (z ^ masks[core])) * 2 + (hi ^ flip)
                perm.append(((core * 4 + z) * 2 + hi, there))
    return lax.ppermute(x, ("core", "z", "xhi"), perm)


def join_kernel(a_ref, b_ref, out_ref, sems):
    rows = a_ref.shape[0]
    copies = [
        pltpu.make_async_copy(ref, out_ref.at[pl.ds(i * rows, rows)], sems.at[i])
        for i, ref in enumerate((a_ref, b_ref))
    ]
    for c in copies:
        c.start()
    for c in copies:
        c.wait()


def join(a, b):
    return pl.pallas_call(
        join_kernel,
        in_specs=[ANY, ANY],
        out_specs=ANY,
        out_shape=jax.ShapeDtypeStruct((2 * a.shape[0],) + a.shape[1:], a.dtype),
        scratch_shapes=[pltpu.SemaphoreType.DMA((2,))],
        compiler_params=grant(2),
        name="join",
    )(a, b)


def scale_of(pieces, width):
    total = jnp.sum(pieces[0] * pieces[0], axis=-1, keepdims=True)
    for piece in pieces[1:]:
        total = total + jnp.sum(piece * piece, axis=-1, keepdims=True)
    return lax.rsqrt(total / width + norm_eps)


def head_norm(values):
    return values * lax.rsqrt(jnp.mean(values * values, axis=-1, keepdims=True) + norm_eps)


def project_kernel(n, me_ref, *refs):
    pairs = refs[: n // 2]
    gain, qg, kg, cos, sin = refs[n // 2 : n // 2 + 5]
    hbm, (q_out, kv_out) = refs[n // 2 + 5 : n // 2 + 8], refs[n // 2 + 8 : n // 2 + 10]
    (wq, wk, wv), sems = refs[n // 2 + 10 : -1], refs[-1]
    copies = [
        pltpu.make_async_copy(src, dst, sems.at[i])
        for i, (src, dst) in enumerate(zip(hbm, (wq, wk, wv)))
    ]
    for c in copies:
        c.start()
    me = me_ref[2]
    width = pairs[0].shape[2]
    hd = qg.shape[1]
    xs = [p[i].astype(F32) for p in pairs for i in range(2)]
    scale = scale_of(xs, n * width)
    for c in copies:
        c.wait()
    q = k = v = None
    for step in range(n):
        src = jnp.bitwise_xor(me, step)
        rows = pl.ds(pl.multiple_of(src * width, width), width)
        x = (xs[step] * scale * gain[rows].astype(F32)[None, :]).astype(BF16)
        dq = jnp.dot(x, wq[rows, :], preferred_element_type=F32)
        dk = jnp.dot(x, wk[rows, :], preferred_element_type=F32)
        dv = jnp.dot(x, wv[rows, :], preferred_element_type=F32)
        q, k, v = (dq, dk, dv) if q is None else (q + dq, k + dk, v + dv)
    c = cos[...].reshape(q.shape[0], hd)
    s = sin[...].reshape(q.shape[0], hd)
    for h in range(q.shape[1] // hd):
        part = q[:, h * hd : (h + 1) * hd]
        q_out[:, h * hd : (h + 1) * hd] = rotate(head_norm(part) * qg[...], c, s).astype(BF16)
    kv_out[:, :hd] = rotate(head_norm(k) * kg[...], c, s).astype(BF16)
    kv_out[:, hd:] = v.astype(BF16)


def identity(rows, cols, period):
    row = lax.broadcasted_iota(jnp.int32, (rows, cols), 0)
    col = lax.broadcasted_iota(jnp.int32, (rows, cols), 1)
    return jnp.where(lax.rem(row, period) == col, 1.0, 0.0).astype(BF16)


def attend_kernel(count, ids, tab, kpos, k_index, q_index, cos, sin, *refs):
    q_in, kv_in, cached = refs[0:4], refs[4:8], refs[8:12]
    outs = refs[12:16]
    keys, values, new_keys, queries, bounds, places, run_m, run_l, run_acc, todo, sems = refs[16:]
    hd = keys.shape[2]
    span = cached[0].shape[1]
    slots = keys.shape[0]
    place_at = tab.shape[0] // 2
    xy, mk = ids[0], ids[1]
    copies = []
    for p in range(4):
        for which, dst in enumerate((keys, values)):
            copies.append(
                pltpu.make_async_copy(
                    cached[p].at[pl.ds(2 * which, 2)],
                    dst.at[pl.ds(2 * p, 2), pl.ds(0, span), :],
                    sems.at[which, p],
                )
            )
    for c in copies:
        c.start()

    key_rows = []
    for ki in range(slots):
        k_nat = jnp.bitwise_xor(mk, ki // 2) * 2 + ki % 2
        k_slot = xy * 8 + k_nat
        key_rows.append((tab[k_slot], tab[place_at + k_slot], ki * 8 + k_nat * 64))
    found = jnp.int32(0)
    for qi in range(slots):
        p = qi // 2
        q_slot = jnp.bitwise_xor(xy, p) * 8 + jnp.bitwise_xor(mk, (p % 2) * 2) * 2 + qi % 2
        q_req, q_place = tab[q_slot], tab[place_at + q_slot]
        for k_req, k_place, word in key_rows:
            todo[found] = word + qi + jnp.where(k_place < q_place, 512, 0)
            seen = jnp.logical_and(k_req == q_req, k_place <= q_place)
            found = found + seen.astype(jnp.int32)
    todo[found] = 1024

    def entry(at):
        word = todo[at]
        return word % 8, word // 8 % 8, word // 64 % 8, word // 512

    pad = values.shape[1] - span - count
    for p in range(4):
        for j in range(2):
            fresh = kv_in[p][j * count : (j + 1) * count, :]
            zero = jnp.zeros((pad, hd), BF16)
            new_keys[2 * p + j] = jnp.concatenate([fresh[:, :hd], zero], 0)
            values[2 * p + j, span:, :] = jnp.concatenate([fresh[:, hd:], zero], 0)
            rows = q_in[p][j * count : (j + 1) * count, :]
            queries[2 * p + j] = jnp.concatenate([rows[:, :hd], rows[:, hd:]], 0)
    places[:, :span] = kpos[...]
    places[:, span:] = jnp.concatenate(
        [k_index[...].astype(F32), jnp.full((slots, pad), FAR, F32)], axis=1
    )
    index = q_index[...].astype(F32)
    upper = jnp.floor(index * 0.125)
    digits = jnp.concatenate([upper, index - 8.0 * upper], 0).astype(BF16)
    columns = lax.dot_general(
        identity(2 * count, count, count),
        digits,
        (((1,), (1,)), ((), ())),
        preferred_element_type=F32,
    )
    for q in range(slots):
        bounds[q] = 8.0 * columns[:, q : q + 1] + columns[:, slots + q : slots + q + 1]
    run_m[...] = jnp.full(run_m.shape, NEG, F32)
    run_l[...] = jnp.zeros(run_l.shape, F32)
    run_acc[...] = jnp.zeros(run_acc.shape, F32)
    for c in copies:
        c.wait()
    factor = hd**-0.5 * math.log2(math.e)

    def score(at):
        qi, ki, k_nat, _ = entry(at)
        row = pl.ds(k_nat, 1)
        query = queries[qi]
        turned = rotate(query.astype(F32), cos[row, :], sin[row, :]).astype(BF16)
        return jnp.concatenate(
            [
                lax.dot_general(
                    q, k[ki], (((1,), (1,)), ((), ())), preferred_element_type=F32
                )
                for q, k in ((turned, keys), (query, new_keys))
            ],
            axis=1,
        )

    def soften(at, scores):
        qi, _, k_nat, level = entry(at)
        offset = jnp.where(level == 1, 65536.0, jnp.where(level == 2, -65536.0, 0.0))
        bound = bounds[qi] + offset
        scores = jnp.where(places[pl.ds(k_nat, 1), :] <= bound, scores, NEG)
        old = run_m[qi]
        new = jnp.maximum(old, jnp.max(scores, axis=-1, keepdims=True))
        shrink = jnp.exp2((old - new) * factor)
        weights = jnp.exp2((scores - new) * factor)
        run_m[qi] = new
        run_l[qi] = run_l[qi] * shrink + jnp.sum(weights, axis=-1, keepdims=True)
        return shrink, weights.astype(BF16)

    def gather(at, shrink, weights):
        qi, ki, _, _ = entry(at)
        run_acc[qi] = run_acc[qi] * shrink + jnp.dot(
            weights, values[ki], preferred_element_type=F32
        )

    def two(i, _):
        first, second = 2 * i, 2 * i + 1
        s1 = score(first)
        s2 = score(second)
        soft1 = soften(first, s1)
        soft2 = soften(second, s2)
        gather(first, *soft1)
        gather(second, *soft2)
        return 0

    lax.fori_loop(0, (found + 1) // 2, two, 0)

    lane = lax.broadcasted_iota(jnp.int32, (2 * count, hd), 1)
    dest, entry, level = lane // 16, lane % 4, (lane % 16) // 4
    stats = jnp.zeros((2 * count, hd), F32)
    for p in range(4):
        for j in range(2):
            stats = jnp.where((dest == p) & (entry == j), run_m[2 * p + j], stats)
            stats = jnp.where((dest == p) & (entry == 2 + j), run_l[2 * p + j], stats)
    high = stats.astype(BF16).astype(F32)
    mid = (stats - high).astype(BF16).astype(F32)
    low = stats - high - mid
    stats = jnp.where(level == 0, high, jnp.where(level == 1, mid, low)).astype(BF16)
    flat = lax.dot_general(
        stats,
        identity(2 * count, 2 * hd, 4 * count),
        (((0,), (0,)), ((), ())),
        preferred_element_type=F32,
    ).astype(BF16)
    for p in range(4):
        for j in range(2):
            outs[p][j, : 2 * count, :] = run_acc[2 * p + j].astype(BF16)
            outs[p][j, 2 * count :, :] = flat[16 * p : 16 * p + 16, j * hd : (j + 1) * hd]


def attend(ids, table, kpos, key_index, query_index, cos, sin, queries, fresh, cached):
    count = query_index.shape[1]
    slot_local = cached[0].shape[0] // 2
    span, hd = cached[0].shape[1:]
    key_rows = span + 128
    return pl.pallas_call(
        functools.partial(attend_kernel, count),
        in_specs=[SMEM, SMEM] + [VMEM] * 13 + [ANY] * 4,
        out_specs=[VMEM] * 4,
        out_shape=[jax.ShapeDtypeStruct((slot_local, 2 * count + 16, hd), BF16)] * 4,
        scratch_shapes=[
            pltpu.VMEM((8, span, hd), BF16),
            pltpu.VMEM((8, key_rows, hd), BF16),
            pltpu.VMEM((8, key_rows - span, hd), BF16),
            pltpu.VMEM((8, 2 * count, hd), BF16),
            pltpu.VMEM((8, 2 * count, 1), F32),
            pltpu.VMEM((8, key_rows), F32),
            pltpu.VMEM((8, 2 * count, 1), F32),
            pltpu.VMEM((8, 2 * count, 1), F32),
            pltpu.VMEM((8, 2 * count, hd), F32),
            pltpu.SMEM((72,), jnp.int32),
            pltpu.SemaphoreType.DMA((2, 4)),
        ],
        compiler_params=grant(18),
        name="attend",
    )(ids, table, kpos, key_index, query_index, cos, sin, *queries, *fresh, *cached)


def merge_kernel(count, *refs):
    parts, out = refs[:4], refs[4]
    hd = parts[0].shape[2]
    turn = identity(2 * count, 2 * hd, 4 * count)
    tops, sums = [], []
    for part in parts:
        flat = jnp.concatenate([part[0, 2 * count :, :], part[1, 2 * count :, :]], axis=1)
        st = lax.dot_general(
            turn, flat, (((1,), (1,)), ((), ())), preferred_element_type=F32
        )
        st = st[:, 0:4] + st[:, 4:8] + st[:, 8:12]
        tops.append(st[:, 0:2])
        sums.append(st[:, 2:4])
    top = functools.reduce(jnp.maximum, tops)
    shares = [jnp.exp((m - top) * hd**-0.5) for m in tops]
    total = functools.reduce(jnp.add, [w * s for w, s in zip(shares, sums)])
    shares = [w / total for w in shares]
    rows = [[], []]
    for j in range(2):
        acc = functools.reduce(
            jnp.add,
            [
                w[:, j : j + 1] * part[j, : 2 * count, :].astype(F32)
                for w, part in zip(shares, parts)
            ],
        )
        for h in range(2):
            rows[h].append(acc[h * count : (h + 1) * count])
    out[...] = jnp.concatenate([jnp.concatenate(r, 0) for r in rows], 1).astype(BF16)


def feed_kernel(n, ids, *refs):
    pieces, pairs = refs[:n], refs[n : n + n // 2]
    wo_own = refs[n + n // 2 : 2 * n]
    wo_sibling = refs[2 * n : 2 * n + n // 2]
    gain, wg, wu, wd = refs[2 * n + n // 2 : 2 * n + n // 2 + 4]
    outs, mine = refs[2 * n + n // 2 + 4 : -2], refs[-2]
    stream = refs[-1]
    me, core = ids[2], ids[3]
    width = pieces[0].shape[1]
    half = width // 2
    total = None
    for weights, which in ((wo_own, core), (wo_sibling, 1 - core)):
        cols = pl.ds(pl.multiple_of(which * half, half), half)
        for i, weight in enumerate(weights):
            x = jnp.concatenate([pieces[2 * i][:, cols], pieces[2 * i + 1][:, cols]], axis=1)
            part = jnp.dot(x, weight[...], preferred_element_type=F32)
            total = part if total is None else total + part
    stream[...] = total
    for step in range(n):
        src = jnp.bitwise_xor(me, step)
        cols = pl.ds(pl.multiple_of(src * width, width), width)
        stream[:, cols] = stream[:, cols] + pairs[step // 2][step % 2].astype(F32)
        if step == 0:
            mine[...] = stream[:, cols].astype(BF16)
    xs = stream[...].astype(BF16).astype(F32)
    scale = scale_of([xs], n * width)
    x = (xs * scale * gain[...].astype(F32)[None, :]).astype(BF16)
    g = jnp.dot(x, wg[...], preferred_element_type=F32)
    u = jnp.dot(x, wu[...], preferred_element_type=F32)
    active = (g / (1.0 + jnp.exp(-g)) * u).astype(BF16)
    for step in range(n):
        src = jnp.bitwise_xor(me, step)
        cols = pl.ds(pl.multiple_of(src * width, width), width)
        outs[step][...] = jnp.dot(active, wd[:, cols], preferred_element_type=F32).astype(BF16)


def on_device(
    selected_hidden,
    cached_keys,
    cached_values,
    slot_spans,
    span_order,
    cache_start,
    selected_index,
    input_gain,
    query_weight,
    key_weight,
    value_weight,
    query_gain,
    key_gain,
    output_weight,
    post_gain,
    gate_weight,
    up_weight,
    down_weight,
):
    slot_local, count, width = selected_hidden.shape
    span = cached_keys.shape[1]
    hd = query_gain.shape[0]
    rows = slot_local * count
    spans = span_order.shape[1]
    n = 8

    def shaped(*shape, dtype=BF16):
        return jax.ShapeDtypeStruct(shape, dtype)

    def rows_at(array, start, size):
        return lax.dynamic_slice(array, (start, 0), (size, array.shape[1]), allow_negative_indices=False)

    hidden = selected_hidden.reshape(rows, width)
    half = output_weight.shape[0] // 2
    xy = lax.axis_index(("xlo", "yhi"))
    core = lax.axis_index("core")
    seq = lax.axis_index(SEQ)
    ids = jnp.stack([xy, lax.axis_index(("ylo", "core")), lax.axis_index(TP), core])

    number = lax.broadcasted_iota(jnp.int32, span_order.shape, 0) * spans
    number = number + lax.broadcasted_iota(jnp.int32, span_order.shape, 1)
    hit = slot_spans[:, None, None] == number[None]
    place = jnp.sum(jnp.where(hit, span_order[None], 0), axis=(1, 2))
    start = jnp.sum(jnp.where(hit, cache_start[None], 0), axis=(1, 2))
    table = jnp.concatenate([slot_spans // spans, place])

    pair = jnp.stack([hidden, swap(hidden, "xhi", 1, 2)])

    output_half = rows_at(output_weight, core * half, half)
    cached_keys, place = lax.optimization_barrier((cached_keys, place))
    cached = join(cached_keys, cached_values)
    cached_y = swap(cached, "ylo", 1, 2)
    cached_core = swap(cached, "core", 1, 2)

    (
        pair,
        cached_core,
        selected_later,
        place,
        start,
        ids,
        at_group,
        *at_slots,
    ) = lax.optimization_barrier(
        (pair, cached_core, selected_index, place, start, ids, xy * 8)
        + tuple(jnp.bitwise_xor(seq, 2 * k) * slot_local for k in (0,) + FAR_MASKS)
    )
    output_x = swap(output_half, "xhi", 1, 2)
    pairs = [pair] + [swap(pair, "z", k, 4) for k in (1, 2, 3)]

    base_here = rows_at((place * span)[:, None], at_slots[0], slot_local)
    index_here = rows_at(selected_later, at_slots[0], slot_local)
    qc, qs = rotation_tables(base_here + index_here, hd)
    qg, kg = query_gain.astype(F32)[None], key_gain.astype(F32)[None]
    output_half, output_x, pairs[1] = lax.optimization_barrier(
        (output_half, output_x, pairs[1])
    )
    wo_0 = join(output_half, output_x)
    wo_1 = cross(wo_0, 1, 0)
    pairs[0], qg, kg, qc, qs, ids, table = lax.optimization_barrier(
        (pairs[0], qg, kg, qc, qs, ids, table)
    )
    queries, fresh = pl.pallas_call(
        functools.partial(project_kernel, n),
        in_specs=[SMEM] + [VMEM] * (n // 2 + 5) + [HBM] * 3,
        out_specs=[VMEM, VMEM],
        scratch_shapes=[
            pltpu.VMEM(w.shape, BF16) for w in (query_weight, key_weight, value_weight)
        ]
        + [pltpu.SemaphoreType.DMA((3,))],
        out_shape=[shaped(rows, query_weight.shape[1]), shaped(rows, 2 * hd)],
        compiler_params=grant(10),
        name="project",
    )(
        ids,
        *pairs,
        input_gain,
        qg,
        kg,
        qc,
        qs,
        query_weight,
        key_weight,
        value_weight,
    )
    cached_y, selected_last, start, _ = lax.optimization_barrier(
        (cached_y, selected_later, start, fresh)
    )
    cached_set = [cached, cached_core, cached_y, swap(cached_y, "core", 1, 2)]
    fresh_y = swap(fresh, "ylo", 1, 2)
    fresh_set = [fresh, swap(fresh, "core", 1, 2), fresh_y, swap(fresh_y, "core", 1, 2)]
    query_set = [queries] + [swap(queries, ROUND, k, 8) for k in FAR_MASKS]

    group_index = rows_at(selected_last, at_group, 8)
    token = jnp.arange(span, dtype=jnp.int32)
    taken = jnp.any(group_index[:, :, None] == token[None, None, :], axis=1)
    kpos = jnp.where(taken, FAR, token[None, :].astype(F32))
    query_index = jnp.concatenate(
        [rows_at(selected_last, at, slot_local) for at in at_slots], axis=0
    )
    query_set[1], wo_1 = lax.optimization_barrier((query_set[1], wo_1))
    wo_2 = cross(wo_0, 2, 0)
    wo_3 = cross(wo_1, 2, 0)
    wo_0, wo_1, query_set[3] = lax.optimization_barrier((wo_0, wo_1, query_set[3]))
    wo_0c, wo_1c = swap(wo_0, "core", 1, 2), swap(wo_1, "core", 1, 2)

    shift = rows_at((place * span - start)[:, None], at_group, 8)[:, 0]
    kc, ks = rotation_tables(-shift, hd)
    parts = attend(
        ids,
        table,
        kpos,
        group_index,
        query_index,
        kc,
        ks,
        query_set,
        fresh_set,
        cached_set,
    )
    *parts, wo_0c, wo_1c = lax.optimization_barrier((*parts, wo_0c, wo_1c))
    parts = [parts[0]] + [swap(part, ROUND, k, 8) for part, k in zip(parts[1:], FAR_MASKS)]

    attended = pl.pallas_call(
        functools.partial(merge_kernel, count),
        in_specs=[VMEM] * 4,
        out_specs=VMEM,
        out_shape=shaped(rows, width),
        compiler_params=grant(8),
        name="merge",
    )(*parts)
    order = [(3, 1), (1, 1), (2, 1), (3, 0), (0, 1), (1, 0), (2, 0)]
    wo_2, wo_3, attended = lax.optimization_barrier((wo_2, wo_3, attended))
    wo_2c, wo_3c = swap(wo_2, "core", 1, 2), swap(wo_3, "core", 1, 2)
    wo_own = [wo_0, wo_1, wo_2, wo_3]
    wo_2c, wo_3c, later = lax.optimization_barrier((wo_2c, wo_3c, attended))
    pieces = [attended] + [None] * (n - 1)
    for i, (kind, flip) in enumerate(order):
        pieces[2 * kind + flip] = cross(attended if i < 3 else later, kind, flip)
    *downs, stream = pl.pallas_call(
        functools.partial(feed_kernel, n),
        in_specs=[SMEM] + [VMEM] * (2 * n + n // 2 + 4),
        out_specs=[VMEM] * (n + 1),
        out_shape=[shaped(rows, width)] * (n + 1),
        scratch_shapes=[pltpu.VMEM((rows, n * width), F32)],
        compiler_params=grant(20),
        name="feed",
    )(
        ids,
        *pieces,
        *pairs,
        *wo_own,
        wo_0c,
        wo_2c,
        wo_1c,
        wo_3c,
        post_gain,
        gate_weight,
        up_weight,
        down_weight,
    )
    total = stream.astype(F32) + downs[0].astype(F32)
    for k in (5, 3, 7, 4, 1, 2, 6):
        total = total + swap(downs[k], TP, k, n).astype(F32)
    return total.astype(BF16).reshape(slot_local, count, width)


def solution(mesh):
    fine = Mesh(
        mesh.devices.reshape(2, 2, 2, 2, 4, 2), ("xlo", "yhi", "ylo", "core", "z", "xhi")
    )
    in_specs = (
        P(SEQ, None, TP),
        P(SEQ, None, TP),
        P(SEQ, None, TP),
        P(),
        P(),
        P(),
        P(),
        P(),
        P(None, TP),
        P(None, TP),
        P(None, TP),
        P(),
        P(),
        P(TP, None),
        P(),
        P(None, TP),
        P(None, TP),
        P(TP, None),
    )
    return jax.shard_map(
        on_device, mesh=fine, in_specs=in_specs, out_specs=P(SEQ, None, TP), check_vma=False
    )
```

```python
import functools
import math

import jax
import jax.numpy as jnp
from jax import lax
from jax.experimental import pallas as pl
from jax.experimental.pallas import tpu as pltpu
from jax.sharding import Mesh
from jax.sharding import PartitionSpec as P

theta_base = 1000000.0
norm_eps = 1e-06
NEG = -1e30
FAR = 1e9
TP = ("z", "xhi")
SEQ = ("xlo", "yhi", "ylo", "core")
ROUND = ("xlo", "yhi", "ylo")
FAR_MASKS = (3, 4, 7)
VMEM = pl.BlockSpec(memory_space=pltpu.VMEM)
SMEM = pl.BlockSpec(memory_space=pltpu.SMEM)
ANY = pl.BlockSpec(memory_space=pl.ANY)
HBM = pl.BlockSpec(memory_space=pltpu.HBM)
F32 = jnp.float32
BF16 = jnp.bfloat16


def rotation_tables(positions, head_dim):
    half = head_dim // 2
    frequency = jnp.exp(-jnp.log(theta_base) * jnp.arange(half, dtype=F32) * 2.0 / head_dim)
    angles = positions.astype(F32)[..., None] * frequency
    cosine, sine = jnp.cos(angles), jnp.sin(angles)
    return jnp.concatenate([cosine, cosine], -1), jnp.concatenate([-sine, sine], -1)


def rotate(values, cosine, sine):
    return values * cosine + pltpu.roll(values, values.shape[-1] // 2, values.ndim - 1) * sine


def grant(mib):
    return pltpu.CompilerParams(vmem_limit_bytes=mib << 20)


def swap(x, axes, mask, size):
    return lax.ppermute(x, axes, [(i, i ^ mask) for i in range(size)])


def cross(x, kind, flip):
    masks = {0: (0, 0), 1: (1, 3), 2: (3, 1), 3: (2, 2)}[kind]
    perm = []
    for core in range(2):
        for z in range(4):
            for hi in range(2):
                there = (core * 4 + (z ^ masks[core])) * 2 + (hi ^ flip)
                perm.append(((core * 4 + z) * 2 + hi, there))
    return lax.ppermute(x, ("core", "z", "xhi"), perm)


def join_kernel(a_ref, b_ref, out_ref, sems):
    rows = a_ref.shape[0]
    copies = [
        pltpu.make_async_copy(ref, out_ref.at[pl.ds(i * rows, rows)], sems.at[i])
        for i, ref in enumerate((a_ref, b_ref))
    ]
    for c in copies:
        c.start()
    for c in copies:
        c.wait()


def join(a, b):
    return pl.pallas_call(
        join_kernel,
        in_specs=[ANY, ANY],
        out_specs=ANY,
        out_shape=jax.ShapeDtypeStruct((2 * a.shape[0],) + a.shape[1:], a.dtype),
        scratch_shapes=[pltpu.SemaphoreType.DMA((2,))],
        compiler_params=grant(2),
        name="join",
    )(a, b)


def scale_of(pieces, width):
    total = jnp.sum(pieces[0] * pieces[0], axis=-1, keepdims=True)
    for piece in pieces[1:]:
        total = total + jnp.sum(piece * piece, axis=-1, keepdims=True)
    return lax.rsqrt(total / width + norm_eps)


def head_norm(values):
    return values * lax.rsqrt(jnp.mean(values * values, axis=-1, keepdims=True) + norm_eps)


def project_kernel(n, me_ref, *refs):
    pairs = refs[: n // 2]
    gain, qg, kg, cos, sin = refs[n // 2 : n // 2 + 5]
    hbm, (q_out, kv_out) = refs[n // 2 + 5 : n // 2 + 8], refs[n // 2 + 8 : n // 2 + 10]
    (wq, wk, wv), sems = refs[n // 2 + 10 : -1], refs[-1]
    copies = [
        pltpu.make_async_copy(src, dst, sems.at[i])
        for i, (src, dst) in enumerate(zip(hbm, (wq, wk, wv)))
    ]
    for c in copies:
        c.start()
    me = me_ref[2]
    width = pairs[0].shape[2]
    hd = qg.shape[1]
    xs = [p[i].astype(F32) for p in pairs for i in range(2)]
    scale = scale_of(xs, n * width)
    for c in copies:
        c.wait()
    q = k = v = None
    for step in range(n):
        src = jnp.bitwise_xor(me, step)
        rows = pl.ds(pl.multiple_of(src * width, width), width)
        x = (xs[step] * scale * gain[rows].astype(F32)[None, :]).astype(BF16)
        dq = jnp.dot(x, wq[rows, :], preferred_element_type=F32)
        dk = jnp.dot(x, wk[rows, :], preferred_element_type=F32)
        dv = jnp.dot(x, wv[rows, :], preferred_element_type=F32)
        q, k, v = (dq, dk, dv) if q is None else (q + dq, k + dk, v + dv)
    factor = hd**-0.5 * math.log2(math.e)
    c = cos[...].reshape(q.shape[0], hd)
    s = sin[...].reshape(q.shape[0], hd)
    for h in range(q.shape[1] // hd):
        part = q[:, h * hd : (h + 1) * hd]
        q_out[:, h * hd : (h + 1) * hd] = (rotate(head_norm(part) * qg[...], c, s) * factor).astype(BF16)
    kv_out[:, :hd] = rotate(head_norm(k) * kg[...], c, s).astype(BF16)
    kv_out[:, hd:] = v.astype(BF16)


def identity(rows, cols, period):
    row = lax.broadcasted_iota(jnp.int32, (rows, cols), 0)
    col = lax.broadcasted_iota(jnp.int32, (rows, cols), 1)
    return jnp.where(lax.rem(row, period) == col, 1.0, 0.0).astype(BF16)


def attend_kernel(count, ids, tab, kpos, k_index, q_index, cos, sin, *refs):
    q_in, kv_in, cached = refs[0:4], refs[4:8], refs[8:12]
    outs = refs[12:16]
    keys, values, new_keys, queries, bounds, places, run_m, run_l, run_acc, todo, sems = refs[16:]
    hd = keys.shape[2]
    span = cached[0].shape[1]
    slots = keys.shape[0]
    place_at = tab.shape[0] // 2
    xy, mk = ids[0], ids[1]
    copies = []
    for p in range(4):
        for which, dst in enumerate((keys, values)):
            copies.append(
                pltpu.make_async_copy(
                    cached[p].at[pl.ds(2 * which, 2)],
                    dst.at[pl.ds(2 * p, 2), pl.ds(0, span), :],
                    sems.at[which, p],
                )
            )
    for c in copies:
        c.start()

    key_rows = []
    for ki in range(slots):
        k_nat = jnp.bitwise_xor(mk, ki // 2) * 2 + ki % 2
        k_slot = xy * 8 + k_nat
        key_rows.append((tab[k_slot], tab[place_at + k_slot], ki * 8 + k_nat * 64))
    found = jnp.int32(0)
    for qi in range(slots):
        p = qi // 2
        q_slot = jnp.bitwise_xor(xy, p) * 8 + jnp.bitwise_xor(mk, (p % 2) * 2) * 2 + qi % 2
        q_req, q_place = tab[q_slot], tab[place_at + q_slot]
        for k_req, k_place, word in key_rows:
            todo[found] = word + qi + jnp.where(k_place < q_place, 512, 0)
            seen = jnp.logical_and(k_req == q_req, k_place <= q_place)
            found = found + seen.astype(jnp.int32)
    todo[found] = 1024

    def entry(at):
        word = todo[at]
        return word % 8, word // 8 % 8, word // 64 % 8, word // 512

    pad = values.shape[1] - span - count
    for p in range(4):
        for j in range(2):
            fresh = kv_in[p][j * count : (j + 1) * count, :]
            zero = jnp.zeros((pad, hd), BF16)
            new_keys[2 * p + j] = jnp.concatenate([fresh[:, :hd], zero], 0)
            values[2 * p + j, span:, :] = jnp.concatenate([fresh[:, hd:], zero], 0)
            rows = q_in[p][j * count : (j + 1) * count, :]
            queries[2 * p + j] = jnp.concatenate([rows[:, :hd], rows[:, hd:]], 0)
    places[:, :span] = kpos[...]
    places[:, span:] = jnp.concatenate(
        [k_index[...].astype(F32), jnp.full((slots, pad), FAR, F32)], axis=1
    )
    index = q_index[...].astype(F32)
    upper = jnp.floor(index * 0.125)
    digits = jnp.concatenate([upper, index - 8.0 * upper], 0).astype(BF16)
    columns = lax.dot_general(
        identity(2 * count, count, count),
        digits,
        (((1,), (1,)), ((), ())),
        preferred_element_type=F32,
    )
    for q in range(slots):
        bounds[q] = 8.0 * columns[:, q : q + 1] + columns[:, slots + q : slots + q + 1]
    run_m[...] = jnp.full(run_m.shape, NEG, F32)
    run_l[...] = jnp.zeros(run_l.shape, F32)
    run_acc[...] = jnp.zeros(run_acc.shape, F32)
    for c in copies:
        c.wait()

    def score(at):
        qi, ki, k_nat, _ = entry(at)
        row = pl.ds(k_nat, 1)
        query = queries[qi]
        turned = rotate(query.astype(F32), cos[row, :], sin[row, :]).astype(BF16)
        return jnp.concatenate(
            [
                lax.dot_general(
                    q, k[ki], (((1,), (1,)), ((), ())), preferred_element_type=F32
                )
                for q, k in ((turned, keys), (query, new_keys))
            ],
            axis=1,
        )

    def soften(at, scores):
        qi, _, k_nat, level = entry(at)
        offset = jnp.where(level == 1, 65536.0, jnp.where(level == 2, -65536.0, 0.0))
        bound = bounds[qi] + offset
        scores = jnp.where(places[pl.ds(k_nat, 1), :] <= bound, scores, NEG)
        old = run_m[qi]
        new = jnp.maximum(old, jnp.max(scores, axis=-1, keepdims=True))
        shrink = jnp.exp2(old - new)
        weights = jnp.exp2(scores - new)
        run_m[qi] = new
        run_l[qi] = run_l[qi] * shrink + jnp.sum(weights, axis=-1, keepdims=True)
        return shrink, weights.astype(BF16)

    def gather(at, shrink, weights):
        qi, ki, _, _ = entry(at)
        run_acc[qi] = run_acc[qi] * shrink + jnp.dot(
            weights, values[ki], preferred_element_type=F32
        )

    def two(i, _):
        first, second = 2 * i, 2 * i + 1
        s1 = score(first)
        s2 = score(second)
        soft1 = soften(first, s1)
        soft2 = soften(second, s2)
        gather(first, *soft1)
        gather(second, *soft2)
        return 0

    lax.fori_loop(0, (found + 1) // 2, two, 0)

    lane = lax.broadcasted_iota(jnp.int32, (2 * count, hd), 1)
    dest, entry, level = lane // 16, lane % 4, (lane % 16) // 4
    stats = jnp.zeros((2 * count, hd), F32)
    for p in range(4):
        for j in range(2):
            stats = jnp.where((dest == p) & (entry == j), run_m[2 * p + j], stats)
            stats = jnp.where((dest == p) & (entry == 2 + j), run_l[2 * p + j], stats)
    high = stats.astype(BF16).astype(F32)
    mid = (stats - high).astype(BF16).astype(F32)
    low = stats - high - mid
    stats = jnp.where(level == 0, high, jnp.where(level == 1, mid, low)).astype(BF16)
    flat = lax.dot_general(
        stats,
        identity(2 * count, 2 * hd, 4 * count),
        (((0,), (0,)), ((), ())),
        preferred_element_type=F32,
    ).astype(BF16)
    for p in range(4):
        for j in range(2):
            outs[p][j, : 2 * count, :] = run_acc[2 * p + j].astype(BF16)
            outs[p][j, 2 * count :, :] = flat[16 * p : 16 * p + 16, j * hd : (j + 1) * hd]


def attend(ids, table, kpos, key_index, query_index, cos, sin, queries, fresh, cached):
    count = query_index.shape[1]
    slot_local = cached[0].shape[0] // 2
    span, hd = cached[0].shape[1:]
    key_rows = span + 128
    return pl.pallas_call(
        functools.partial(attend_kernel, count),
        in_specs=[SMEM, SMEM] + [VMEM] * 13 + [ANY] * 4,
        out_specs=[VMEM] * 4,
        out_shape=[jax.ShapeDtypeStruct((slot_local, 2 * count + 16, hd), BF16)] * 4,
        scratch_shapes=[
            pltpu.VMEM((8, span, hd), BF16),
            pltpu.VMEM((8, key_rows, hd), BF16),
            pltpu.VMEM((8, key_rows - span, hd), BF16),
            pltpu.VMEM((8, 2 * count, hd), BF16),
            pltpu.VMEM((8, 2 * count, 1), F32),
            pltpu.VMEM((8, key_rows), F32),
            pltpu.VMEM((8, 2 * count, 1), F32),
            pltpu.VMEM((8, 2 * count, 1), F32),
            pltpu.VMEM((8, 2 * count, hd), F32),
            pltpu.SMEM((72,), jnp.int32),
            pltpu.SemaphoreType.DMA((2, 4)),
        ],
        compiler_params=grant(18),
        name="attend",
    )(ids, table, kpos, key_index, query_index, cos, sin, *queries, *fresh, *cached)


def merge_kernel(count, *refs):
    parts, out = refs[:4], refs[4]
    hd = parts[0].shape[2]
    turn = identity(2 * count, 2 * hd, 4 * count)
    tops, sums = [], []
    for part in parts:
        flat = jnp.concatenate([part[0, 2 * count :, :], part[1, 2 * count :, :]], axis=1)
        st = lax.dot_general(
            turn, flat, (((1,), (1,)), ((), ())), preferred_element_type=F32
        )
        st = st[:, 0:4] + st[:, 4:8] + st[:, 8:12]
        tops.append(st[:, 0:2])
        sums.append(st[:, 2:4])
    top = functools.reduce(jnp.maximum, tops)
    shares = [jnp.exp2(m - top) for m in tops]
    total = functools.reduce(jnp.add, [w * s for w, s in zip(shares, sums)])
    shares = [w / total for w in shares]
    rows = [[], []]
    for j in range(2):
        acc = functools.reduce(
            jnp.add,
            [
                w[:, j : j + 1] * part[j, : 2 * count, :].astype(F32)
                for w, part in zip(shares, parts)
            ],
        )
        for h in range(2):
            rows[h].append(acc[h * count : (h + 1) * count])
    out[...] = jnp.concatenate([jnp.concatenate(r, 0) for r in rows], 1).astype(BF16)


def feed_kernel(n, ids, *refs):
    pieces, pairs = refs[:n], refs[n : n + n // 2]
    wo_own = refs[n + n // 2 : 2 * n]
    wo_sibling = refs[2 * n : 2 * n + n // 2]
    gain, wg, wu, wd = refs[2 * n + n // 2 : 2 * n + n // 2 + 4]
    outs, mine = refs[2 * n + n // 2 + 4 : -2], refs[-2]
    stream = refs[-1]
    me, core = ids[2], ids[3]
    width = pieces[0].shape[1]
    half = width // 2
    total = None
    for weights, which in ((wo_own, core), (wo_sibling, 1 - core)):
        cols = pl.ds(pl.multiple_of(which * half, half), half)
        for i, weight in enumerate(weights):
            x = jnp.concatenate([pieces[2 * i][:, cols], pieces[2 * i + 1][:, cols]], axis=1)
            part = jnp.dot(x, weight[...], preferred_element_type=F32)
            total = part if total is None else total + part
    stream[...] = total
    for step in range(n):
        src = jnp.bitwise_xor(me, step)
        cols = pl.ds(pl.multiple_of(src * width, width), width)
        stream[:, cols] = stream[:, cols] + pairs[step // 2][step % 2].astype(F32)
        if step == 0:
            mine[...] = stream[:, cols].astype(BF16)
    xs = stream[...].astype(BF16).astype(F32)
    scale = scale_of([xs], n * width)
    x = (xs * scale * gain[...].astype(F32)[None, :]).astype(BF16)
    g = jnp.dot(x, wg[...], preferred_element_type=F32)
    u = jnp.dot(x, wu[...], preferred_element_type=F32)
    active = (g / (1.0 + jnp.exp(-g)) * u).astype(BF16)
    for step in range(n):
        src = jnp.bitwise_xor(me, step)
        cols = pl.ds(pl.multiple_of(src * width, width), width)
        outs[step][...] = jnp.dot(active, wd[:, cols], preferred_element_type=F32).astype(BF16)


def on_device(
    selected_hidden,
    cached_keys,
    cached_values,
    slot_spans,
    span_order,
    cache_start,
    selected_index,
    input_gain,
    query_weight,
    key_weight,
    value_weight,
    query_gain,
    key_gain,
    output_weight,
    post_gain,
    gate_weight,
    up_weight,
    down_weight,
):
    slot_local, count, width = selected_hidden.shape
    span = cached_keys.shape[1]
    hd = query_gain.shape[0]
    rows = slot_local * count
    spans = span_order.shape[1]
    n = 8

    def shaped(*shape, dtype=BF16):
        return jax.ShapeDtypeStruct(shape, dtype)

    def rows_at(array, start, size):
        return lax.dynamic_slice(array, (start, 0), (size, array.shape[1]), allow_negative_indices=False)

    hidden = selected_hidden.reshape(rows, width)
    half = output_weight.shape[0] // 2
    xy = lax.axis_index(("xlo", "yhi"))
    core = lax.axis_index("core")
    seq = lax.axis_index(SEQ)
    ids = jnp.stack([xy, lax.axis_index(("ylo", "core")), lax.axis_index(TP), core])

    number = lax.broadcasted_iota(jnp.int32, span_order.shape, 0) * spans
    number = number + lax.broadcasted_iota(jnp.int32, span_order.shape, 1)
    hit = slot_spans[:, None, None] == number[None]
    place = jnp.sum(jnp.where(hit, span_order[None], 0), axis=(1, 2))
    start = jnp.sum(jnp.where(hit, cache_start[None], 0), axis=(1, 2))
    table = jnp.concatenate([slot_spans // spans, place])

    pair = jnp.stack([hidden, swap(hidden, "xhi", 1, 2)])

    output_half = rows_at(output_weight, core * half, half)
    cached_keys, place = lax.optimization_barrier((cached_keys, place))
    cached = join(cached_keys, cached_values)
    cached_y = swap(cached, "ylo", 1, 2)
    cached_core = swap(cached, "core", 1, 2)

    (
        pair,
        cached_core,
        selected_later,
        place,
        start,
        ids,
        at_group,
        *at_slots,
    ) = lax.optimization_barrier(
        (pair, cached_core, selected_index, place, start, ids, xy * 8)
        + tuple(jnp.bitwise_xor(seq, 2 * k) * slot_local for k in (0,) + FAR_MASKS)
    )
    output_x = swap(output_half, "xhi", 1, 2)
    pairs = [pair] + [swap(pair, "z", k, 4) for k in (1, 2, 3)]

    base_here = rows_at((place * span)[:, None], at_slots[0], slot_local)
    index_here = rows_at(selected_later, at_slots[0], slot_local)
    qc, qs = rotation_tables(base_here + index_here, hd)
    qg, kg = query_gain.astype(F32)[None], key_gain.astype(F32)[None]
    output_half, output_x, pairs[1] = lax.optimization_barrier(
        (output_half, output_x, pairs[1])
    )
    wo_0 = join(output_half, output_x)
    wo_1 = cross(wo_0, 1, 0)
    pairs[0], qg, kg, qc, qs, ids, table = lax.optimization_barrier(
        (pairs[0], qg, kg, qc, qs, ids, table)
    )
    queries, fresh = pl.pallas_call(
        functools.partial(project_kernel, n),
        in_specs=[SMEM] + [VMEM] * (n // 2 + 5) + [HBM] * 3,
        out_specs=[VMEM, VMEM],
        scratch_shapes=[
            pltpu.VMEM(w.shape, BF16) for w in (query_weight, key_weight, value_weight)
        ]
        + [pltpu.SemaphoreType.DMA((3,))],
        out_shape=[shaped(rows, query_weight.shape[1]), shaped(rows, 2 * hd)],
        compiler_params=grant(10),
        name="project",
    )(
        ids,
        *pairs,
        input_gain,
        qg,
        kg,
        qc,
        qs,
        query_weight,
        key_weight,
        value_weight,
    )
    cached_y, selected_last, start, _ = lax.optimization_barrier(
        (cached_y, selected_later, start, fresh)
    )
    cached_set = [cached, cached_core, cached_y, swap(cached_y, "core", 1, 2)]
    fresh_y = swap(fresh, "ylo", 1, 2)
    fresh_set = [fresh, swap(fresh, "core", 1, 2), fresh_y, swap(fresh_y, "core", 1, 2)]
    query_set = [queries] + [swap(queries, ROUND, k, 8) for k in FAR_MASKS]

    group_index = rows_at(selected_last, at_group, 8)
    token = jnp.arange(span, dtype=jnp.int32)
    taken = jnp.any(group_index[:, :, None] == token[None, None, :], axis=1)
    kpos = jnp.where(taken, FAR, token[None, :].astype(F32))
    query_index = jnp.concatenate(
        [rows_at(selected_last, at, slot_local) for at in at_slots], axis=0
    )
    query_set[1], wo_1 = lax.optimization_barrier((query_set[1], wo_1))
    wo_2 = cross(wo_0, 2, 0)
    wo_3 = cross(wo_1, 2, 0)
    wo_0, wo_1, query_set[3] = lax.optimization_barrier((wo_0, wo_1, query_set[3]))
    wo_0c, wo_1c = swap(wo_0, "core", 1, 2), swap(wo_1, "core", 1, 2)

    shift = rows_at((place * span - start)[:, None], at_group, 8)[:, 0]
    kc, ks = rotation_tables(-shift, hd)
    parts = attend(
        ids,
        table,
        kpos,
        group_index,
        query_index,
        kc,
        ks,
        query_set,
        fresh_set,
        cached_set,
    )
    *parts, wo_0c, wo_1c = lax.optimization_barrier((*parts, wo_0c, wo_1c))
    parts = [parts[0]] + [swap(part, ROUND, k, 8) for part, k in zip(parts[1:], FAR_MASKS)]

    attended = pl.pallas_call(
        functools.partial(merge_kernel, count),
        in_specs=[VMEM] * 4,
        out_specs=VMEM,
        out_shape=shaped(rows, width),
        compiler_params=grant(8),
        name="merge",
    )(*parts)
    order = [(3, 1), (1, 1), (2, 1), (3, 0), (0, 1), (1, 0), (2, 0)]
    wo_2, wo_3, attended = lax.optimization_barrier((wo_2, wo_3, attended))
    wo_2c, wo_3c = swap(wo_2, "core", 1, 2), swap(wo_3, "core", 1, 2)
    wo_own = [wo_0, wo_1, wo_2, wo_3]
    wo_2c, wo_3c, later = lax.optimization_barrier((wo_2c, wo_3c, attended))
    pieces = [attended] + [None] * (n - 1)
    for i, (kind, flip) in enumerate(order):
        pieces[2 * kind + flip] = cross(attended if i < 3 else later, kind, flip)
    *downs, stream = pl.pallas_call(
        functools.partial(feed_kernel, n),
        in_specs=[SMEM] + [VMEM] * (2 * n + n // 2 + 4),
        out_specs=[VMEM] * (n + 1),
        out_shape=[shaped(rows, width)] * (n + 1),
        scratch_shapes=[pltpu.VMEM((rows, n * width), F32)],
        compiler_params=grant(20),
        name="feed",
    )(
        ids,
        *pieces,
        *pairs,
        *wo_own,
        wo_0c,
        wo_2c,
        wo_1c,
        wo_3c,
        post_gain,
        gate_weight,
        up_weight,
        down_weight,
    )
    total = stream.astype(F32) + downs[0].astype(F32)
    for k in (5, 3, 7, 4, 1, 2, 6):
        total = total + swap(downs[k], TP, k, n).astype(F32)
    return total.astype(BF16).reshape(slot_local, count, width)


def solution(mesh):
    fine = Mesh(
        mesh.devices.reshape(2, 2, 2, 2, 4, 2), ("xlo", "yhi", "ylo", "core", "z", "xhi")
    )
    in_specs = (
        P(SEQ, None, TP),
        P(SEQ, None, TP),
        P(SEQ, None, TP),
        P(),
        P(),
        P(),
        P(),
        P(),
        P(None, TP),
        P(None, TP),
        P(None, TP),
        P(),
        P(),
        P(TP, None),
        P(),
        P(None, TP),
        P(None, TP),
        P(TP, None),
    )
    return jax.shard_map(
        on_device, mesh=fine, in_specs=in_specs, out_specs=P(SEQ, None, TP), check_vma=False
    )
```
